32 devices in a mesh: groups: 2 (over y), wake: 4 (over x, core), panel: 4 (over z).
Axes of the slice: x: 2, y: 2, z: 4, core: 2. Of those that a mesh axis runs over, the one named last changes fastest.
Arguments:
- positions: float32 [3, 4096], P(None, ('groups', 'wake', 'panel')), parts along dimension 1, may hold values from -1 to 1
- strengths: float32 [3, 4096], P(None, ('groups', 'wake', 'panel')), parts along dimension 1, may hold values from -0.24 to 0.24
- cores: float32 [1, 4096], P(None, ('groups', 'wake', 'panel')), parts along dimension 1, may hold values from 0.05 to 0.2
- panel_centers: float32 [3, 32768], P(None, ('groups', 'wake', 'panel')), parts along dimension 1, may hold values from -1 to 1
- panel_normals: float32 [3, 32768], P(None, ('groups', 'wake', 'panel')), parts along dimension 1, may hold values from -1 to 1, as said below
- panel_areas: float32 [1, 32768], P(None, ('groups', 'wake', 'panel')), parts along dimension 1, may hold values from 0.004 to 0.04
- influence: float32 [32768, 16384], P(('groups', 'wake'), 'panel'), parts along dimension 0, may hold values from -1 to 2.5
- blade_ids: int32 [32768], P(('groups', 'wake', 'panel')), parts along dimension 0, may hold values from 0 to 3
- blade_velocity: float32 [8, 3], P('groups'), parts along dimension 0, may hold values from -4 to 4
Outputs:
- velocity: float32 [3, 4096], P(None, ('groups', 'wake', 'panel')), parts along dimension 1
- stretching: float32 [3, 4096], P(None, ('groups', 'wake', 'panel')), parts along dimension 1
- panel_strengths: float32 [32768], P(('groups', 'wake', 'panel')), parts along dimension 0
The draws below stay inside these ranges and needn't reach their ends.
There are 2 independent parts, one for each index of `groups`. The reference program is written for one: setup_inputs(seed, part) draws one part's arguments, and reference() takes and returns one part's arrays. A program takes and returns all parts, laid end to end along the dimension named above; each array names one. Nothing has to cross between parts.
Inputs may be any that keep to these rules, and one draw needn't show every extreme that they name: `panel_normals`: each column has unit length.
All inputs are finite; a program needn't handle non-finite values.
Results may differ from the reference program's by a relative error of at most 0.0003.
Values sent between devices are 32-bit elements; how exact they have to be, the bound alone decides.
No kernel may reach another device: no remote copies, remote signals or barrier semaphores. Data moves between devices by JAX's collectives and lax.ppermute only.
A program may use at most 128 MiB of HBM per device.

```python
import math
import jax
import jax.numpy as jnp
from jax import lax

NP = 16384
BLADES = 4
ITERS = 4
NPART = 2048


def draw_panel_normals(key, part):
    first, second = jax.random.split(jax.random.fold_in(key, 11))
    height = jax.random.uniform(first, (NP,), jnp.float32, -1.0, 1.0)
    turning = jax.random.uniform(second, (NP,), jnp.float32, -math.pi, math.pi)
    radius = jnp.sqrt(jnp.maximum(1.0 - height * height, 0.0))
    return jnp.stack([radius * jnp.cos(turning), radius * jnp.sin(turning), height])


def draw_influence(key, part):
    first, second = jax.random.split(jax.random.fold_in(key, 23))
    spread = jnp.clip(jax.random.normal(first, (NP, NP), jnp.float32), -6.0, 6.0) * (0.5 / math.sqrt(NP))
    diagonal = jax.random.uniform(second, (NP,), jnp.float32, 1.5, 2.5)
    indices = jnp.arange(NP, dtype=jnp.int32)
    return spread.at[indices, indices].set(diagonal)


def set_ends(entries, stream_key, smallest, high):
    place = [jax.random.randint(jax.random.fold_in(stream_key, axis), (), 0, length) for axis, length in enumerate(entries.shape)]
    widest = entries.shape.index(max(entries.shape))
    neighbour = place[:widest] + [(place[widest] + 1) % entries.shape[widest]] + place[widest + 1:]
    return entries.at[tuple(place)].set(smallest).at[tuple(neighbour)].set(high)


def block_scale(rng, extent, cuts, low, largest):
    level = 1.0
    for position, parts in cuts:
        heights = jax.random.uniform(jax.random.fold_in(jax.random.fold_in(rng, 6), position), (parts,), jnp.float32, low / len(cuts), largest / len(cuts))
        level = level * jnp.repeat(jnp.exp(heights), extent[position] // parts).reshape((-1,) + (1,) * (len(extent) - 1 - position))
    return level


def bell_draw(own_key, shape, width, reach, cuts=(), kind=jnp.bfloat16):
    result = jax.random.normal(own_key, shape, jnp.float32) * width
    if len(cuts) > 0:
        result = block_scale(own_key, shape, cuts, -0.22, 0.18) * result
    return jnp.clip(result, min=-reach, max=reach).astype(kind)


def setup_inputs(seed: int = 0, part: int = 0) -> dict:
    keys = jax.random.split(jax.random.key(seed), 10)
    own_keys = jax.random.split(jax.random.fold_in(keys[9], part), 10)
    return {
        "positions": jnp.clip(jax.random.uniform(own_keys[0], (3, NPART), jnp.float32, -1.0, 1.0) * block_scale(own_keys[0], (3, NPART), ((1, 16),), -0.4, 0.0), -1.0, 1.0),
        "strengths": bell_draw(own_keys[1], (3, NPART), 0.04, 0.24, ((1, 16),), jnp.float32),
        "cores": jnp.clip(jnp.exp(math.log(0.2) - 1.3862944 * jax.random.uniform(own_keys[2], (1, NPART), jnp.float32) ** block_scale(own_keys[2], (1, NPART), ((1, 16),), -0.2, 0.2)), 0.05, 0.2),
        "panel_centers": jnp.clip(jax.random.uniform(own_keys[3], (3, NP), jnp.float32, -1.0, 1.0) * block_scale(own_keys[3], (3, NP), ((1, 16),), -0.4, 0.0), -1.0, 1.0),
        "panel_normals": draw_panel_normals(jax.random.fold_in(jax.random.fold_in(keys[9], part), 71), part),
        "panel_areas": jnp.clip(jnp.exp(math.log(0.04) - 2.30258502 * jax.random.uniform(own_keys[5], (1, NP), jnp.float32) ** block_scale(own_keys[5], (1, NP), ((1, 16),), -0.2, 0.2)), 0.004, 0.04),
        "influence": draw_influence(jax.random.fold_in(jax.random.fold_in(keys[9], part), 71), part),
        "blade_ids": set_ends(jax.random.randint(own_keys[7], (NP,), 0, BLADES), jax.random.fold_in(own_keys[7], 1), 0, BLADES - 1).astype(jnp.int32),
        "blade_velocity": bell_draw(own_keys[8], (BLADES, 3), 1.0, 4.0, (), jnp.float32),
    }


inv_four_pi = 1.0 / (4.0 * math.pi)
relax_factor = 0.5
freestream = (0.0, 0.0, -1.0)

def vortex_terms(targets, sources):
    target_pos, target_str, target_core = targets
    source_pos, source_str, source_core = sources
    offset_x = target_pos[0][:, None] - source_pos[0][None, :]
    offset_y = target_pos[1][:, None] - source_pos[1][None, :]
    offset_z = target_pos[2][:, None] - source_pos[2][None, :]
    core_sq = 0.5 * (target_core[0][:, None] * target_core[0][:, None] + source_core[0][None, :] * source_core[0][None, :])
    distance = offset_x * offset_x + offset_y * offset_y + offset_z * offset_z + core_sq
    inverse = lax.rsqrt(distance)
    falloff = inverse * inverse * inverse
    steeper = falloff * inverse * inverse
    source_x = source_str[0][None, :]
    source_y = source_str[1][None, :]
    source_z = source_str[2][None, :]
    target_x = target_str[0][:, None]
    target_y = target_str[1][:, None]
    target_z = target_str[2][:, None]
    cross_x = offset_y * source_z - offset_z * source_y
    cross_y = offset_z * source_x - offset_x * source_z
    cross_z = offset_x * source_y - offset_y * source_x
    twist_x = target_y * source_z - target_z * source_y
    twist_y = target_z * source_x - target_x * source_z
    twist_z = target_x * source_y - target_y * source_x
    along = 3.0 * steeper * (target_x * offset_x + target_y * offset_y + target_z * offset_z)
    return jnp.stack([lax.optimization_barrier(jnp.sum(falloff * cross_x, axis=1)), lax.optimization_barrier(jnp.sum(falloff * cross_y, axis=1)), lax.optimization_barrier(jnp.sum(falloff * cross_z, axis=1)), lax.optimization_barrier(jnp.sum(falloff * twist_x - along * cross_x, axis=1)), lax.optimization_barrier(jnp.sum(falloff * twist_y - along * cross_y, axis=1)), lax.optimization_barrier(jnp.sum(falloff * twist_z - along * cross_z, axis=1))])

def wake_terms(targets, sources):
    points = targets[0]
    source_pos, source_str, source_core = sources
    offset_x = points[0][:, None] - source_pos[0][None, :]
    offset_y = points[1][:, None] - source_pos[1][None, :]
    offset_z = points[2][:, None] - source_pos[2][None, :]
    distance = offset_x * offset_x + offset_y * offset_y + offset_z * offset_z + source_core[0][None, :] * source_core[0][None, :]
    inverse = lax.rsqrt(distance)
    falloff = inverse * inverse * inverse
    source_x = source_str[0][None, :]
    source_y = source_str[1][None, :]
    source_z = source_str[2][None, :]
    return jnp.stack([lax.optimization_barrier(jnp.sum(falloff * (offset_y * source_z - offset_z * source_y), axis=1)), lax.optimization_barrier(jnp.sum(falloff * (offset_z * source_x - offset_x * source_z), axis=1)), lax.optimization_barrier(jnp.sum(falloff * (offset_x * source_y - offset_y * source_x), axis=1))])

def panel_terms(targets, sources):
    points = targets[0]
    centers, weights, areas = sources
    offset_x = points[0][:, None] - centers[0][None, :]
    offset_y = points[1][:, None] - centers[1][None, :]
    offset_z = points[2][:, None] - centers[2][None, :]
    distance = offset_x * offset_x + offset_y * offset_y + offset_z * offset_z + 4.0 * areas[0][None, :]
    inverse = lax.rsqrt(distance)
    weighted = weights[0][None, :] * inverse * inverse * inverse
    return jnp.stack([lax.optimization_barrier(jnp.sum(weighted * offset_x, axis=1)), lax.optimization_barrier(jnp.sum(weighted * offset_y, axis=1)), lax.optimization_barrier(jnp.sum(weighted * offset_z, axis=1))])

def tiles(array):
    return jnp.moveaxis(array.reshape(array.shape[0], -1, 128), 1, 0)

def untile(array):
    return jnp.moveaxis(array, 0, 1).reshape(array.shape[1], -1)

def reference(positions, strengths, cores, panel_centers, panel_normals, panel_areas, influence, blade_ids, blade_velocity):
    sources = (positions, strengths, cores)
    pair_sums = untile(lax.map(lambda entry: vortex_terms(entry, sources), (tiles(positions), tiles(strengths), tiles(cores))))
    wake_velocity = -inv_four_pi * untile(lax.map(lambda entry: wake_terms(entry, sources), (tiles(panel_centers),)))
    onehot = (blade_ids[None, :] == jnp.arange(BLADES, dtype=jnp.int32)[:, None]).astype(jnp.float32)
    kinematic = jnp.dot(blade_velocity.T, onehot, precision=lax.Precision.HIGHEST)
    onset = jnp.asarray(freestream, jnp.float32)[:, None] + kinematic + wake_velocity
    right_side = -lax.optimization_barrier(jnp.sum(panel_normals * onset, axis=0))
    panel_strengths = relax_factor * right_side
    for turn in range(ITERS - 1):
        image = jnp.dot(influence, panel_strengths, precision=lax.Precision.HIGHEST)
        panel_strengths = panel_strengths + relax_factor * (right_side - image)
    weights = (panel_strengths * panel_areas[0])[None, :]
    panel_sources = (panel_centers, weights, panel_areas)
    panel_sums = untile(lax.map(lambda entry: panel_terms(entry, panel_sources), (tiles(positions),)))
    velocity = jnp.asarray(freestream, jnp.float32)[:, None] - inv_four_pi * pair_sums[:3] + inv_four_pi * panel_sums
    stretching = -inv_four_pi * pair_sums[3:]
    return (velocity, stretching, panel_strengths)
```

```python
import functools
import math

import jax
import jax.numpy as jnp
from jax import lax
from jax.experimental import pallas as pl
from jax.experimental.pallas import tpu as pltpu
from jax.sharding import PartitionSpec as P

BLADES = 4
ITERS = 4


inv_four_pi = 1.0 / (4.0 * math.pi)
relax_factor = 0.5
freestream = (0.0, 0.0, -1.0)
block_width = 2048


def spread(block, axis, source):
    block = jnp.where(lax.axis_index(axis) == source, block, jnp.zeros_like(block))
    return lax.psum(block, axis)


def vortex_terms(targets, sources):
    target_pos, target_str, target_core = targets
    source_pos, source_str, source_core = sources
    offset_x = target_pos[0][:, None] - source_pos[0][None, :]
    offset_y = target_pos[1][:, None] - source_pos[1][None, :]
    offset_z = target_pos[2][:, None] - source_pos[2][None, :]
    core_sq = 0.5 * (
        target_core[0][:, None] * target_core[0][:, None]
        + source_core[0][None, :] * source_core[0][None, :]
    )
    distance = offset_x * offset_x + offset_y * offset_y + offset_z * offset_z + core_sq
    inverse = lax.rsqrt(distance)
    falloff = inverse * inverse * inverse
    steeper = falloff * inverse * inverse
    source_x = source_str[0][None, :]
    source_y = source_str[1][None, :]
    source_z = source_str[2][None, :]
    target_x = target_str[0][:, None]
    target_y = target_str[1][:, None]
    target_z = target_str[2][:, None]
    cross_x = offset_y * source_z - offset_z * source_y
    cross_y = offset_z * source_x - offset_x * source_z
    cross_z = offset_x * source_y - offset_y * source_x
    twist_x = target_y * source_z - target_z * source_y
    twist_y = target_z * source_x - target_x * source_z
    twist_z = target_x * source_y - target_y * source_x
    along = 3.0 * steeper * (target_x * offset_x + target_y * offset_y + target_z * offset_z)
    return jnp.stack(
        [
            jnp.sum(falloff * cross_x, axis=1),
            jnp.sum(falloff * cross_y, axis=1),
            jnp.sum(falloff * cross_z, axis=1),
            jnp.sum(falloff * twist_x - along * cross_x, axis=1),
            jnp.sum(falloff * twist_y - along * cross_y, axis=1),
            jnp.sum(falloff * twist_z - along * cross_z, axis=1),
        ]
    )


def wake_terms(targets, sources):
    points = targets[0]
    source_pos, source_str, source_core = sources
    offset_x = points[0][:, None] - source_pos[0][None, :]
    offset_y = points[1][:, None] - source_pos[1][None, :]
    offset_z = points[2][:, None] - source_pos[2][None, :]
    distance = (
        offset_x * offset_x
        + offset_y * offset_y
        + offset_z * offset_z
        + source_core[0][None, :] * source_core[0][None, :]
    )
    inverse = lax.rsqrt(distance)
    falloff = inverse * inverse * inverse
    source_x = source_str[0][None, :]
    source_y = source_str[1][None, :]
    source_z = source_str[2][None, :]
    return jnp.stack(
        [
            jnp.sum(falloff * (offset_y * source_z - offset_z * source_y), axis=1),
            jnp.sum(falloff * (offset_z * source_x - offset_x * source_z), axis=1),
            jnp.sum(falloff * (offset_x * source_y - offset_y * source_x), axis=1),
        ]
    )


def panel_terms(targets, sources):
    points = targets[0]
    centers, weights, areas = sources
    offset_x = points[0][:, None] - centers[0][None, :]
    offset_y = points[1][:, None] - centers[1][None, :]
    offset_z = points[2][:, None] - centers[2][None, :]
    distance = (
        offset_x * offset_x + offset_y * offset_y + offset_z * offset_z + 4.0 * areas[0][None, :]
    )
    inverse = lax.rsqrt(distance)
    weighted = weights[0][None, :] * inverse * inverse * inverse
    return jnp.stack(
        [
            jnp.sum(weighted * offset_x, axis=1),
            jnp.sum(weighted * offset_y, axis=1),
            jnp.sum(weighted * offset_z, axis=1),
        ]
    )


def over_sources(kernel, targets, sources, width, out_rows):
    length = sources[0].shape[-1]
    stride = math.gcd(length, width)
    if stride == length:
        return kernel(targets, sources)
    pieces = tuple(
        (
            jnp.moveaxis(source.reshape(source.shape[0], length // stride, stride), 1, 0)
            for source in sources
        )
    )

    def visit(running, entry):
        return (running + kernel(targets, entry), None)

    initial = jnp.zeros((out_rows, targets[0].shape[-1]), jnp.float32)
    running, unused = lax.scan(visit, initial, pieces)
    return running


def column_of(row_block):
    wake_count = lax.axis_size("wake")
    panel_count = lax.axis_size("panel")
    panel_at = lax.axis_index("panel")
    first_root = panel_at * wake_count // panel_count
    donors = max(1, wake_count // panel_count)
    pieces = []
    for offset_rank in range(donors):
        pieces.append(spread(row_block, "wake", first_root + offset_rank))
    joined = pieces[0] if donors == 1 else jnp.concatenate(pieces, axis=0)
    return joined


def relax(right_side, influence):
    row_side = lax.all_gather(right_side, "panel", axis=0, tiled=True)
    current = relax_factor * row_side
    for turn in range(ITERS - 1):
        column = column_of(current)
        partial_value = jnp.dot(influence, column, precision=lax.Precision.HIGHEST)
        image = lax.psum(partial_value, "panel")
        current = current + relax_factor * (row_side - image)
    own_start = lax.axis_index("panel") * right_side.shape[0]
    return lax.dynamic_slice_in_dim(current, own_start, right_side.shape[0], 0)


def plain_device(
    positions,
    strengths,
    cores,
    panel_centers,
    panel_normals,
    panel_areas,
    influence,
    blade_ids,
    blade_velocity,
):
    onset_dir = jnp.asarray(freestream, jnp.float32)[:, None]
    onehot = (blade_ids[None, :] == jnp.arange(BLADES, dtype=jnp.int32)[:, None]).astype(
        jnp.float32
    )
    kinematic = jnp.dot(blade_velocity.T, onehot, precision=lax.Precision.HIGHEST) + onset_dir
    moving = -jnp.sum(panel_normals * kinematic, axis=0)
    particles = (positions, strengths, cores)
    piece = (
        lax.all_gather(positions, ("wake", "panel"), axis=1, tiled=True),
        lax.all_gather(strengths, ("wake", "panel"), axis=1, tiled=True),
        lax.all_gather(cores, ("wake", "panel"), axis=1, tiled=True),
    )
    pair_sums = over_sources(vortex_terms, particles, piece, block_width, 6)
    wake_sums = over_sources(wake_terms, (panel_centers,), piece, block_width, 3)
    right_side = moving + inv_four_pi * jnp.sum(panel_normals * wake_sums, axis=0)
    centers, areas = (
        lax.all_gather(panel_centers, ("wake", "panel"), axis=1, tiled=True),
        lax.all_gather(panel_areas, ("wake", "panel"), axis=1, tiled=True),
    )
    panel_strengths = relax(right_side, influence)
    all_strengths = lax.all_gather(panel_strengths, ("wake", "panel"), axis=0, tiled=True)
    weights = (all_strengths * areas[0])[None, :]
    panel_sums = over_sources(panel_terms, (positions,), (centers, weights, areas), block_width, 3)
    velocity = onset_dir - inv_four_pi * pair_sums[:3] + inv_four_pi * panel_sums
    stretching = -inv_four_pi * pair_sums[3:]
    return (velocity, stretching, panel_strengths)


LANES = 128
MIB = 1 << 20
KEEP_BYTES = 52 * MIB
RING_ROWS = 64
RING = 4
AXES = ("wake", "panel")

vmem = pl.BlockSpec(memory_space=pltpu.VMEM)
smem = pl.BlockSpec(memory_space=pltpu.SMEM)
anywhere = pl.BlockSpec(memory_space=pl.ANY)


def f32(*shape):
    return jax.ShapeDtypeStruct(shape, jnp.float32)


def params(mib):
    return pltpu.CompilerParams(vmem_limit_bytes=mib * MIB)


def send(value, wake_count, panel_count, route):
    pairs = []
    for w in range(wake_count):
        for p in range(panel_count):
            target = route(w, p)
            if target is not None:
                pairs.append((w * panel_count + p, target[0] * panel_count + target[1]))
    return lax.ppermute(value, AXES, pairs)


def pack_kernel(
    positions, strengths, cores, centers, normals, areas, ids, blades, particle_out, mixed_out
):
    particle_out[0:3, :] = positions[...]
    particle_out[3:6, :] = strengths[...]
    particle_out[6:7, :] = cores[...]
    particle_out[7:8, :] = jnp.zeros_like(cores[...])
    width = centers.shape[1]
    mixed_out[0:3, 0:width] = centers[...]
    mixed_out[3:4, 0:width] = areas[...]
    mixed_out[4:7, 0:width] = normals[...]
    owner = ids[...]
    total = None
    for axis in range(3):
        speed = jnp.zeros(owner.shape, jnp.float32)
        for blade in range(BLADES):
            speed = jnp.where(owner == blade, blades[blade, axis], speed)
        term = normals[axis : axis + 1, :] * (speed + freestream[axis])
        total = term if total is None else total + term
    mixed_out[7:8, 0:width] = -total
    mixed_out[:, width:] = particle_out[...]


def load_kernel(row, rows, influence, keep, sem):
    copy = pltpu.make_async_copy(influence.at[pl.ds(row, rows)], keep, sem)
    copy.start()
    copy.wait()


def thirds(value):
    high = value.astype(jnp.bfloat16).astype(jnp.float32)
    rest = value - high
    middle = rest.astype(jnp.bfloat16).astype(jnp.float32)
    return high, middle, rest - middle


def wake_kernel(wake_count, panel_count, row, rows, *refs):
    mixed = refs[:panel_count]
    planes = refs[panel_count : panel_count + wake_count]
    influence, panels, plane, line, partial_out, keep = refs[panel_count + wake_count :][:6]
    left, right, product, spots, running, sem = refs[panel_count + wake_count + 6 :]
    copy = pltpu.make_async_copy(influence.at[pl.ds(row, rows)], keep, sem)
    copy.start()
    w = lax.axis_index("wake")
    p = lax.axis_index("panel")
    nl = planes[0].shape[1]
    m = mixed[0].shape[1] - nl
    for j in range(panel_count):
        at = lax.rem(p + panel_count - j, panel_count)
        panels[:, pl.ds(pl.multiple_of(at * m, LANES), m)] = mixed[j][:, 0:m]
        line[:, pl.ds(pl.multiple_of(at * nl, LANES), nl)] = mixed[j][:, m:]
    for j in range(wake_count):
        at = lax.rem(w + wake_count - j, wake_count)
        plane[:, pl.ds(pl.multiple_of(at * nl, LANES), nl)] = planes[j][...]
    count = plane.shape[1]
    targets = panels.shape[1]
    px, py, pz = (plane[k : k + 1, :] for k in range(3))
    sx, sy, sz = (plane[k : k + 1, :] for k in range(3, 6))
    blank = jnp.zeros((2, count), jnp.float32)
    source = jnp.concatenate(
        [sx, sy, sz, py * sz - pz * sy, pz * sx - px * sz, px * sy - py * sx, blank], axis=0
    )
    high, middle, low = thirds(source)
    left[...] = jnp.concatenate([high, high, middle, high, low, middle], axis=0).T.astype(
        jnp.bfloat16
    )
    cx, cy, cz = (panels[k : k + 1, :] for k in range(3))
    nx, ny, nz = (panels[k : k + 1, :] for k in range(4, 7))
    blank = jnp.zeros((2, targets), jnp.float32)
    target = jnp.concatenate(
        [ny * cz - nz * cy, nz * cx - nx * cz, nx * cy - ny * cx, -nx, -ny, -nz, blank], axis=0
    )
    high, middle, low = thirds(target)
    right[...] = jnp.concatenate([high, middle, high, low, high, middle], axis=0).astype(
        jnp.bfloat16
    )
    for tile in range(count // LANES):
        turned = plane[:, tile * LANES : (tile + 1) * LANES].T
        for k in range(3):
            spots[k, tile * LANES : (tile + 1) * LANES, :] = jnp.broadcast_to(
                turned[:, k : k + 1], (LANES, LANES)
            )
        spots[3, tile * LANES : (tile + 1) * LANES, :] = jnp.broadcast_to(
            turned[:, 6:7] * turned[:, 6:7], (LANES, LANES)
        )
    wide = product.shape[2]
    deep = product.shape[1]
    steps = count // deep
    total = targets // wide * steps

    def multiply(step, slot):
        column = lax.div(step, steps)
        block = lax.rem(step, steps)
        product[slot] = jnp.dot(
            left[pl.ds(pl.multiple_of(block * deep, deep), deep), :],
            right[:, pl.ds(pl.multiple_of(column * wide, wide), wide)],
            preferred_element_type=jnp.float32,
        )

    running[...] = jnp.zeros_like(running)
    multiply(0, 0)

    @pl.loop(0, total)
    def _(step):
        slot = lax.rem(step, 2)
        column = lax.div(step, steps)
        block = lax.rem(step, steps)
        multiply(jnp.minimum(step + 1, total - 1), 1 - slot)
        tiles = wide // LANES
        spot = []
        for t in range(tiles):
            lanes = pl.ds(pl.multiple_of(column * wide + t * LANES, LANES), LANES)
            spot.append(
                tuple(jnp.broadcast_to(panels[k : k + 1, lanes], (8, LANES)) for k in range(3))
            )
        sums = [jnp.zeros((8, LANES), jnp.float32)] * tiles
        for g in range(deep // 8):
            at = pl.ds(pl.multiple_of(block * deep + g * 8, 8), 8)
            qx, qy, qz, core = (spots[k, at, :] for k in range(4))
            for t in range(tiles):
                dx = spot[t][0] - qx
                dy = spot[t][1] - qy
                dz = spot[t][2] - qz
                inverse = lax.rsqrt(dx * dx + dy * dy + (dz * dz + core))
                falloff = inverse * inverse * inverse
                sums[t] = sums[t] + falloff * product[
                    slot, g * 8 : g * 8 + 8, t * LANES : (t + 1) * LANES
                ]
        for t in range(tiles):
            running[column * tiles + t] += sums[t]

    @pl.loop(0, targets // LANES)
    def _(tile):
        partial_out[pl.ds(tile, 1), :] = jnp.sum(running[tile], axis=0, keepdims=True)

    copy.wait()


def pair_kernel(plane, line, out, turned):
    targets = plane.shape[1]
    sources = line.shape[1]
    for tile in range(sources // LANES):
        turned[tile * LANES : (tile + 1) * LANES, :] = line[
            :, tile * LANES : (tile + 1) * LANES
        ].T
    wide = 2

    @pl.loop(0, targets // (wide * LANES))
    def _(column):
        mine = []
        for t in range(wide):
            lanes = pl.ds(pl.multiple_of((column * wide + t) * LANES, LANES), LANES)
            mine.append([jnp.broadcast_to(plane[k : k + 1, lanes], (8, LANES)) for k in range(7)])
            mine[t][6] = 0.5 * (mine[t][6] * mine[t][6])

        def group(g, sums):
            rows = turned[pl.ds(pl.multiple_of(g * 8, 8), 8), :]
            sums = list(sums)
            other = [jnp.broadcast_to(rows[:, k : k + 1], (8, LANES)) for k in range(7)]
            half = 0.5 * (other[6] * other[6])
            for t in range(wide):
                tx, ty, tz, ux, uy, uz, core = mine[t]
                ox, oy, oz, sx, sy, sz, _ = other
                dx, dy, dz = tx - ox, ty - oy, tz - oz
                inverse = lax.rsqrt(dx * dx + dy * dy + dz * dz + (core + half))
                square = inverse * inverse
                falloff = square * inverse
                crosses = (dy * sz - dz * sy, dz * sx - dx * sz, dx * sy - dy * sx)
                twists = (uy * sz - uz * sy, uz * sx - ux * sz, ux * sy - uy * sx)
                along = 3.0 * square * (ux * dx + uy * dy + uz * dz)
                for k in range(3):
                    sums[6 * t + k] += falloff * crosses[k]
                    sums[6 * t + 3 + k] += falloff * (twists[k] - along * crosses[k])
            return tuple(sums)

        zero = jnp.zeros((8, LANES), jnp.float32)
        sums = lax.fori_loop(0, sources // 8, group, (zero,) * (6 * wide), unroll=4)
        for t in range(wide):
            lanes = pl.ds(pl.multiple_of((column * wide + t) * LANES, LANES), LANES)
            for k in range(6):
                out[k : k + 1, lanes] = jnp.sum(sums[6 * t + k], axis=0, keepdims=True)
            out[6:8, lanes] = jnp.zeros((2, LANES), jnp.float32)


def first_kernel(count, *refs):
    partials, (panels, right_side, strengths) = refs[:count], refs[count:]
    wake = partials[0][...]
    for part in partials[1:]:
        wake = wake + part[...]
    right_side[...] = inv_four_pi * wake
    for tile in range(right_side.shape[0]):
        right_side[tile : tile + 1, :] += panels[7:8, tile * LANES : (tile + 1) * LANES]
    strengths[...] = relax_factor * right_side[...]


def next_kernel(count, *refs):
    partials, (right_side, before, strengths) = refs[:count], refs[count:]
    image = partials[0][...]
    for part in partials[1:]:
        image = image + part[...]
    strengths[...] = before[...] + relax_factor * (right_side[...] - image)


def product_kernel(wake_count, panel_count, parts, streamed, *refs):
    blocks = refs[:wake_count]
    keeps = refs[wake_count : wake_count + len(parts)]
    influence, out = refs[wake_count + len(parts) :][:2]
    column, sums, ring, sem = refs[wake_count + len(parts) + 2 :]
    first, rows = streamed
    chunks = rows // RING_ROWS

    def fetch(i):
        return pltpu.make_async_copy(
            influence.at[pl.ds(first + i * RING_ROWS, RING_ROWS)],
            ring.at[i % RING],
            sem.at[i % RING],
        )

    for i in range(min(RING, chunks)):
        fetch(i).start()
    w = lax.axis_index("wake")
    p = lax.axis_index("panel")
    ways = wake_count // panel_count
    height = blocks[0].shape[0]
    for e in range(ways):
        owner = p * ways + e
        value = jnp.zeros(blocks[0].shape, jnp.float32)
        for j in range(wake_count):
            here = lax.rem(w + wake_count - j, wake_count) == owner
            value = value + jnp.where(here, blocks[j][...], 0.0)
        for k in range(height):
            column[e * height + k] = jnp.broadcast_to(value[k : k + 1, :], (8, LANES))
    tiles = column.shape[0]
    vectors = [column[k] for k in range(tiles)]

    def block(ref, start, at, height):
        for g in range(height // 8):
            even = odd = None
            for k in range(0, tiles, 2):
                a = ref[pl.ds(start + 8 * g, 8), k * LANES : (k + 1) * LANES] * vectors[k]
                b = ref[pl.ds(start + 8 * g, 8), (k + 1) * LANES : (k + 2) * LANES] * vectors[k + 1]
                even = a if even is None else even + a
                odd = b if odd is None else odd + b
            sums[pl.ds(at + 8 * g, 8), :] = even + odd

    units = []
    for ref, (start, count) in zip(keeps, parts):
        units.append((ref, start, count // RING_ROWS))
    kept = sum(unit[2] for unit in units)

    def kept_blocks(low, high):
        base = 0
        for ref, start, count in units:
            a, b = max(low, base) - base, min(high, base + count) - base
            if b > a:

                @pl.loop(a, b)
                def _(i, ref=ref, start=start):
                    at = pl.multiple_of(i * RING_ROWS, RING_ROWS)
                    block(ref, at, pl.multiple_of(start + at, RING_ROWS), RING_ROWS)

            base += count

    low = 0
    for i in range(chunks):
        high = kept * (i + 1) // (chunks + 1)
        kept_blocks(low, high)
        low = high
        fetch(i).wait()
        block(ring.at[i % RING], 0, first + i * RING_ROWS, RING_ROWS)
        if i + RING < chunks:
            fetch(i + RING).start()
    kept_blocks(low, kept)
    lane = lax.broadcasted_iota(jnp.int32, (8, LANES), 1)
    diagonal = (lane & 7) == lax.broadcasted_iota(jnp.int32, (8, LANES), 0)

    @pl.loop(0, out.shape[0], unroll=4)
    def _(i):
        gathered = jnp.zeros((8, LANES), jnp.float32)
        for g in range(LANES // 8):
            part = sums[pl.ds(pl.multiple_of(i * LANES + 8 * g, 8), 8), :]
            gathered = jnp.where((lane >> 3) == g, jnp.sum(part, axis=1, keepdims=True), gathered)
        out[pl.ds(i, 1), :] = jnp.sum(jnp.where(diagonal, gathered, 0.0), axis=0, keepdims=True)


def panel_kernel(wake_count, panel_count, *refs):
    blocks = refs[:panel_count]
    panels, plane, pairs = refs[panel_count : panel_count + 3]
    own_out = refs[panel_count + 3]
    outs = refs[panel_count + 4 : panel_count + 4 + wake_count]
    strengths, results = refs[panel_count + 4 + wake_count :]
    w = lax.axis_index("wake")
    p = lax.axis_index("panel")
    root = w // (wake_count // panel_count)
    value = jnp.where(p == root, blocks[0][...], 0.0)
    for block in blocks[1:]:
        value = value + block[...]
    strengths[...] = value
    own = own_out.shape[0]
    own_out[...] = strengths[pl.ds(pl.multiple_of(p * own, own), own), :]
    tiles = strengths.shape[0]
    targets = plane.shape[1]
    wide = 4 if targets % (4 * LANES) == 0 else 1
    zero = jnp.zeros((8, LANES), jnp.float32)
    for column in range(targets // (wide * LANES)):
        spot = []
        for t in range(wide):
            start = (column * wide + t) * LANES
            spot.append(
                [
                    jnp.broadcast_to(plane[k : k + 1, start : start + LANES], (8, LANES))
                    for k in range(3)
                ]
            )

        def visit(tile, sums):
            sums = list(sums)
            lanes = pl.ds(pl.multiple_of(tile * LANES, LANES), LANES)
            area = panels[3:4, lanes]
            rows = jnp.concatenate(
                [
                    panels[0:3, lanes],
                    4.0 * area,
                    area * strengths[pl.ds(tile, 1), :],
                    jnp.zeros((3, LANES), jnp.float32),
                ],
                axis=0,
            ).T
            for g in range(LANES // 8):
                cx, cy, cz, size, weight = (
                    jnp.broadcast_to(rows[8 * g : 8 * g + 8, k : k + 1], (8, LANES))
                    for k in range(5)
                )
                for t in range(wide):
                    dx = spot[t][0] - cx
                    dy = spot[t][1] - cy
                    dz = spot[t][2] - cz
                    inverse = lax.rsqrt(dx * dx + dy * dy + (dz * dz + size))
                    weighted = weight * inverse * (inverse * inverse)
                    sums[3 * t] += weighted * dx
                    sums[3 * t + 1] += weighted * dy
                    sums[3 * t + 2] += weighted * dz
            return tuple(sums)

        sums = lax.fori_loop(0, tiles, visit, (zero,) * (3 * wide))
        for t in range(wide):
            start = (column * wide + t) * LANES
            for k in range(3):
                results[k : k + 1, start : start + LANES] = inv_four_pi * (
                    jnp.sum(sums[3 * t + k], axis=0, keepdims=True)
                    - pairs[k : k + 1, start : start + LANES]
                )
    results[3:6, :] = -inv_four_pi * pairs[3:6, :]
    results[6:8, :] = jnp.zeros_like(pairs[6:8, :])
    nl = outs[0].shape[1]
    for j in range(wake_count):
        at = lax.rem(w + j, wake_count)
        outs[j][...] = results[:, pl.ds(pl.multiple_of(at * nl, LANES), nl)]


def final_kernel(count, *refs):
    parts, (velocity, stretching) = refs[:count], refs[count:]
    total = parts[0][...]
    for part in parts[1:]:
        total = total + part[...]
    for axis in range(3):
        velocity[axis : axis + 1, :] = total[axis : axis + 1, :] + freestream[axis]
    stretching[...] = total[3:6, :]


def block_device(
    positions,
    strengths,
    cores,
    panel_centers,
    panel_normals,
    panel_areas,
    influence,
    blade_ids,
    blade_velocity,
):
    wake_count = lax.axis_size("wake")
    panel_count = lax.axis_size("panel")
    ways = wake_count // panel_count
    nl = positions.shape[1]
    m = panel_centers.shape[1]
    rows, columns = influence.shape
    tiles = rows // LANES
    row_bytes = 4 * columns
    most = min(rows, KEEP_BYTES // row_bytes // LANES * LANES)
    half = most // 2 // LANES * LANES
    parts = ((0, half), (half, most - half))
    streamed = (most, rows - most)
    hold = lambda count: pltpu.VMEM((count, columns), jnp.float32)
    stay = lambda value: pltpu.with_memory_space_constraint(value, pltpu.VMEM)
    route = functools.partial(send, wake_count=wake_count, panel_count=panel_count)

    particle, mixed = pl.pallas_call(
        pack_kernel,
        out_shape=(f32(8, nl), f32(8, m + nl)),
        in_specs=[vmem] * 7 + [smem],
        out_specs=(vmem, vmem),
        compiler_params=params(2),
    )(
        positions,
        strengths,
        cores,
        panel_centers,
        panel_normals,
        panel_areas,
        blade_ids[None, :],
        blade_velocity,
    )
    lines = [mixed] + [
        route(mixed, route=lambda w, p, j=j: (w, (p + j) % panel_count))
        for j in range(1, panel_count)
    ]
    planes = [particle] + [
        route(particle, route=lambda w, p, j=j: ((w + j) % wake_count, p))
        for j in range(1, wake_count)
    ]
    keep_a = pl.pallas_call(
        functools.partial(load_kernel, *parts[0]),
        out_shape=hold(parts[0][1]),
        in_specs=[anywhere],
        out_specs=vmem,
        scratch_shapes=[pltpu.SemaphoreType.DMA],
        compiler_params=params(1),
    )(influence)
    deep = math.gcd(wake_count * nl, 512)
    wide = 2 * LANES if rows % (2 * LANES) == 0 else LANES
    panels, plane, line, partial_sum, keep_b = pl.pallas_call(
        functools.partial(wake_kernel, wake_count, panel_count, *parts[1]),
        out_shape=(
            f32(8, rows),
            f32(8, wake_count * nl),
            f32(8, panel_count * nl),
            f32(tiles, LANES),
            hold(parts[1][1]),
        ),
        in_specs=[vmem] * (panel_count + wake_count) + [anywhere],
        out_specs=(vmem,) * 5,
        scratch_shapes=[
            pltpu.VMEM((wake_count * nl, 48), jnp.bfloat16),
            pltpu.VMEM((48, rows), jnp.bfloat16),
            pltpu.VMEM((2, deep, wide), jnp.float32),
            pltpu.VMEM((4, wake_count * nl, LANES), jnp.float32),
            pltpu.VMEM((tiles, 8, LANES), jnp.float32),
            pltpu.SemaphoreType.DMA,
        ],
        compiler_params=params(9),
    )(*lines, *planes, influence)

    def gather_root(value):
        return [value] + [
            route(
                value,
                route=lambda w, p, j=j: (w, w // ways)
                if p == (w // ways + j) % panel_count
                else None,
            )
            for j in range(1, panel_count)
        ]

    def spread_wake(value):
        return [value] + [
            route(
                value,
                route=lambda w, p, j=j: ((w + j) % wake_count, p) if p == w // ways else None,
            )
            for j in range(1, wake_count)
        ]

    def spread_panel(value):
        return [value] + [
            route(
                value,
                route=lambda w, p, j=j: (w, (p + j) % panel_count) if p == w // ways else None,
            )
            for j in range(1, panel_count)
        ]

    def multiply(blocks):
        return pl.pallas_call(
            functools.partial(product_kernel, wake_count, panel_count, parts, streamed),
            out_shape=f32(tiles, LANES),
            in_specs=[vmem] * (wake_count + len(parts)) + [anywhere],
            out_specs=vmem,
            scratch_shapes=[
                pltpu.VMEM((columns // LANES, 8, LANES), jnp.float32),
                pltpu.VMEM((rows, LANES), jnp.float32),
                pltpu.VMEM((RING, RING_ROWS, columns), jnp.float32),
                pltpu.SemaphoreType.DMA((RING,)),
            ],
            compiler_params=params(7),
        )(*blocks, stay(keep_a), stay(keep_b), influence)

    right_side, current = pl.pallas_call(
        functools.partial(first_kernel, panel_count),
        out_shape=(f32(tiles, LANES), f32(tiles, LANES)),
        in_specs=[vmem] * (panel_count + 1),
        out_specs=(vmem, vmem),
        compiler_params=params(1),
    )(*gather_root(partial_sum), panels)
    pairs = pl.pallas_call(
        pair_kernel,
        out_shape=f32(8, wake_count * nl),
        in_specs=[vmem, vmem],
        out_specs=vmem,
        scratch_shapes=[pltpu.VMEM((panel_count * nl, 8), jnp.float32)],
        compiler_params=params(2),
    )(plane, line)
    for turn in range(ITERS - 1):
        image = multiply(spread_wake(current))
        current = pl.pallas_call(
            functools.partial(next_kernel, panel_count),
            out_shape=f32(tiles, LANES),
            in_specs=[vmem] * (panel_count + 2),
            out_specs=vmem,
            compiler_params=params(1),
        )(*gather_root(image), right_side, current)
    own, *sums = pl.pallas_call(
        functools.partial(panel_kernel, wake_count, panel_count),
        out_shape=(f32(m // LANES, LANES),) + (f32(8, nl),) * wake_count,
        in_specs=[vmem] * (panel_count + 3),
        out_specs=(vmem,) * (1 + wake_count),
        scratch_shapes=[
            pltpu.VMEM((tiles, LANES), jnp.float32),
            pltpu.VMEM((8, wake_count * nl), jnp.float32),
        ],
        compiler_params=params(2),
    )(*spread_panel(current), panels, plane, pairs)
    received = [sums[0]] + [
        route(sums[j], route=lambda w, p, j=j: ((w + j) % wake_count, p))
        for j in range(1, wake_count)
    ]
    velocity, stretching = pl.pallas_call(
        functools.partial(final_kernel, wake_count),
        out_shape=(f32(3, nl), f32(3, nl)),
        in_specs=[vmem] * wake_count,
        out_specs=(vmem, vmem),
        compiler_params=params(1),
    )(*received)
    return (velocity, stretching, own.reshape(m))


def fits(positions, panel_centers, influence):
    wake_count = lax.axis_size("wake")
    panel_count = lax.axis_size("panel")
    return (
        wake_count % panel_count == 0
        and positions.shape[1] % LANES == 0
        and wake_count * positions.shape[1] % (2 * LANES) == 0
        and panel_centers.shape[1] % LANES == 0
        and influence.shape[1] % (2 * LANES) == 0
    )


def per_device(*arrays):
    if fits(arrays[0], arrays[3], arrays[6]):
        return block_device(*arrays)
    return plain_device(*arrays)


def solution(mesh):
    in_specs = (
        P(None, ("groups", "wake", "panel")),
        P(None, ("groups", "wake", "panel")),
        P(None, ("groups", "wake", "panel")),
        P(None, ("groups", "wake", "panel")),
        P(None, ("groups", "wake", "panel")),
        P(None, ("groups", "wake", "panel")),
        P(("groups", "wake"), "panel"),
        P(("groups", "wake", "panel")),
        P("groups", None),
    )
    out_specs = (
        P(None, ("groups", "wake", "panel")),
        P(None, ("groups", "wake", "panel")),
        P(("groups", "wake", "panel")),
    )
    return jax.shard_map(
        per_device, mesh=mesh, in_specs=in_specs, out_specs=out_specs, check_vma=False
    )
```

```python
import functools
import math

import jax
import jax.numpy as jnp
from jax import lax
from jax.experimental import pallas as pl
from jax.experimental.pallas import tpu as pltpu
from jax.sharding import PartitionSpec as P

BLADES = 4
ITERS = 4


inv_four_pi = 1.0 / (4.0 * math.pi)
relax_factor = 0.5
freestream = (0.0, 0.0, -1.0)
block_width = 2048


def spread(block, axis, source):
    block = jnp.where(lax.axis_index(axis) == source, block, jnp.zeros_like(block))
    return lax.psum(block, axis)


def vortex_terms(targets, sources):
    target_pos, target_str, target_core = targets
    source_pos, source_str, source_core = sources
    offset_x = target_pos[0][:, None] - source_pos[0][None, :]
    offset_y = target_pos[1][:, None] - source_pos[1][None, :]
    offset_z = target_pos[2][:, None] - source_pos[2][None, :]
    core_sq = 0.5 * (
        target_core[0][:, None] * target_core[0][:, None]
        + source_core[0][None, :] * source_core[0][None, :]
    )
    distance = offset_x * offset_x + offset_y * offset_y + offset_z * offset_z + core_sq
    inverse = lax.rsqrt(distance)
    falloff = inverse * inverse * inverse
    steeper = falloff * inverse * inverse
    source_x = source_str[0][None, :]
    source_y = source_str[1][None, :]
    source_z = source_str[2][None, :]
    target_x = target_str[0][:, None]
    target_y = target_str[1][:, None]
    target_z = target_str[2][:, None]
    cross_x = offset_y * source_z - offset_z * source_y
    cross_y = offset_z * source_x - offset_x * source_z
    cross_z = offset_x * source_y - offset_y * source_x
    twist_x = target_y * source_z - target_z * source_y
    twist_y = target_z * source_x - target_x * source_z
    twist_z = target_x * source_y - target_y * source_x
    along = 3.0 * steeper * (target_x * offset_x + target_y * offset_y + target_z * offset_z)
    return jnp.stack(
        [
            jnp.sum(falloff * cross_x, axis=1),
            jnp.sum(falloff * cross_y, axis=1),
            jnp.sum(falloff * cross_z, axis=1),
            jnp.sum(falloff * twist_x - along * cross_x, axis=1),
            jnp.sum(falloff * twist_y - along * cross_y, axis=1),
            jnp.sum(falloff * twist_z - along * cross_z, axis=1),
        ]
    )


def wake_terms(targets, sources):
    points = targets[0]
    source_pos, source_str, source_core = sources
    offset_x = points[0][:, None] - source_pos[0][None, :]
    offset_y = points[1][:, None] - source_pos[1][None, :]
    offset_z = points[2][:, None] - source_pos[2][None, :]
    distance = (
        offset_x * offset_x
        + offset_y * offset_y
        + offset_z * offset_z
        + source_core[0][None, :] * source_core[0][None, :]
    )
    inverse = lax.rsqrt(distance)
    falloff = inverse * inverse * inverse
    source_x = source_str[0][None, :]
    source_y = source_str[1][None, :]
    source_z = source_str[2][None, :]
    return jnp.stack(
        [
            jnp.sum(falloff * (offset_y * source_z - offset_z * source_y), axis=1),
            jnp.sum(falloff * (offset_z * source_x - offset_x * source_z), axis=1),
            jnp.sum(falloff * (offset_x * source_y - offset_y * source_x), axis=1),
        ]
    )


def panel_terms(targets, sources):
    points = targets[0]
    centers, weights, areas = sources
    offset_x = points[0][:, None] - centers[0][None, :]
    offset_y = points[1][:, None] - centers[1][None, :]
    offset_z = points[2][:, None] - centers[2][None, :]
    distance = (
        offset_x * offset_x + offset_y * offset_y + offset_z * offset_z + 4.0 * areas[0][None, :]
    )
    inverse = lax.rsqrt(distance)
    weighted = weights[0][None, :] * inverse * inverse * inverse
    return jnp.stack(
        [
            jnp.sum(weighted * offset_x, axis=1),
            jnp.sum(weighted * offset_y, axis=1),
            jnp.sum(weighted * offset_z, axis=1),
        ]
    )


def over_sources(kernel, targets, sources, width, out_rows):
    length = sources[0].shape[-1]
    stride = math.gcd(length, width)
    if stride == length:
        return kernel(targets, sources)
    pieces = tuple(
        (
            jnp.moveaxis(source.reshape(source.shape[0], length // stride, stride), 1, 0)
            for source in sources
        )
    )

    def visit(running, entry):
        return (running + kernel(targets, entry), None)

    initial = jnp.zeros((out_rows, targets[0].shape[-1]), jnp.float32)
    running, unused = lax.scan(visit, initial, pieces)
    return running


def column_of(row_block):
    wake_count = lax.axis_size("wake")
    panel_count = lax.axis_size("panel")
    panel_at = lax.axis_index("panel")
    first_root = panel_at * wake_count // panel_count
    donors = max(1, wake_count // panel_count)
    pieces = []
    for offset_rank in range(donors):
        pieces.append(spread(row_block, "wake", first_root + offset_rank))
    joined = pieces[0] if donors == 1 else jnp.concatenate(pieces, axis=0)
    return joined


def relax(right_side, influence):
    row_side = lax.all_gather(right_side, "panel", axis=0, tiled=True)
    current = relax_factor * row_side
    for turn in range(ITERS - 1):
        column = column_of(current)
        partial_value = jnp.dot(influence, column, precision=lax.Precision.HIGHEST)
        image = lax.psum(partial_value, "panel")
        current = current + relax_factor * (row_side - image)
    own_start = lax.axis_index("panel") * right_side.shape[0]
    return lax.dynamic_slice_in_dim(current, own_start, right_side.shape[0], 0)


def plain_device(
    positions,
    strengths,
    cores,
    panel_centers,
    panel_normals,
    panel_areas,
    influence,
    blade_ids,
    blade_velocity,
):
    onset_dir = jnp.asarray(freestream, jnp.float32)[:, None]
    onehot = (blade_ids[None, :] == jnp.arange(BLADES, dtype=jnp.int32)[:, None]).astype(
        jnp.float32
    )
    kinematic = jnp.dot(blade_velocity.T, onehot, precision=lax.Precision.HIGHEST) + onset_dir
    moving = -jnp.sum(panel_normals * kinematic, axis=0)
    particles = (positions, strengths, cores)
    piece = (
        lax.all_gather(positions, ("wake", "panel"), axis=1, tiled=True),
        lax.all_gather(strengths, ("wake", "panel"), axis=1, tiled=True),
        lax.all_gather(cores, ("wake", "panel"), axis=1, tiled=True),
    )
    pair_sums = over_sources(vortex_terms, particles, piece, block_width, 6)
    wake_sums = over_sources(wake_terms, (panel_centers,), piece, block_width, 3)
    right_side = moving + inv_four_pi * jnp.sum(panel_normals * wake_sums, axis=0)
    centers, areas = (
        lax.all_gather(panel_centers, ("wake", "panel"), axis=1, tiled=True),
        lax.all_gather(panel_areas, ("wake", "panel"), axis=1, tiled=True),
    )
    panel_strengths = relax(right_side, influence)
    all_strengths = lax.all_gather(panel_strengths, ("wake", "panel"), axis=0, tiled=True)
    weights = (all_strengths * areas[0])[None, :]
    panel_sums = over_sources(panel_terms, (positions,), (centers, weights, areas), block_width, 3)
    velocity = onset_dir - inv_four_pi * pair_sums[:3] + inv_four_pi * panel_sums
    stretching = -inv_four_pi * pair_sums[3:]
    return (velocity, stretching, panel_strengths)


LANES = 128
MIB = 1 << 20
KEEP_BYTES = 46 * MIB
SHARES = (24, 12)
SCOPED = 7
RING_ROWS = 64
RING = 4
AXES = ("wake", "panel")

vmem = pl.BlockSpec(memory_space=pltpu.VMEM)
hbm = pl.BlockSpec(memory_space=pltpu.HBM)


def f32(*shape):
    return jax.ShapeDtypeStruct(shape, jnp.float32)


def params(mib):
    return pltpu.CompilerParams(vmem_limit_bytes=mib * MIB)


def send(value, wake_count, panel_count, route):
    pairs = []
    for w in range(wake_count):
        for p in range(panel_count):
            target = route(w, p)
            if target is not None:
                pairs.append((w * panel_count + p, target[0] * panel_count + target[1]))
    return lax.ppermute(value, AXES, pairs)


def pack_kernel(*refs):
    sources, (particle_out, mixed_out), held, sems = refs[:8], refs[8:10], refs[10:18], refs[18]
    copies = [
        pltpu.make_async_copy(source, target, sems.at[i])
        for i, (source, target) in enumerate(zip(sources, held))
    ]
    for copy in copies:
        copy.start()
    for copy in copies:
        copy.wait()
    positions, strengths, cores, centers, normals, areas, ids, blades = held
    particle_out[0:3, :] = positions[...]
    particle_out[3:6, :] = strengths[...]
    particle_out[6:7, :] = cores[...]
    particle_out[7:8, :] = jnp.zeros_like(cores[...])
    width = centers.shape[1]
    mixed_out[0:3, 0:width] = centers[...]
    mixed_out[3:4, 0:width] = areas[...]
    mixed_out[4:7, 0:width] = normals[...]
    owner = ids[...]
    total = None
    for axis in range(3):
        speed = jnp.zeros(owner.shape, jnp.float32)
        for blade in range(BLADES):
            speed = jnp.where(owner == blade, blades[blade, axis], speed)
        term = normals[axis : axis + 1, :] * (speed + freestream[axis])
        total = term if total is None else total + term
    mixed_out[7:8, 0:width] = -total
    mixed_out[:, width:] = particle_out[...]


def thirds(value):
    high = value.astype(jnp.bfloat16).astype(jnp.float32)
    rest = value - high
    middle = rest.astype(jnp.bfloat16).astype(jnp.float32)
    return high, middle, rest - middle


def wake_kernel(wake_count, panel_count, row, rows, *refs):
    mixed = refs[:panel_count]
    planes = refs[panel_count : panel_count + wake_count]
    influence, panels, plane, line, partial_out, keep = refs[panel_count + wake_count :][:6]
    left, right, product, spots, running, sem = refs[panel_count + wake_count + 6 :]
    copy = pltpu.make_async_copy(
        influence.at[pl.ds(row, rows)], keep.at[pl.ds(row, rows)], sem
    )
    copy.start()
    w = lax.axis_index("wake")
    p = lax.axis_index("panel")
    nl = planes[0].shape[1]
    m = mixed[0].shape[1] - nl
    for j in range(panel_count):
        at = lax.rem(p + panel_count - j, panel_count)
        panels[:, pl.ds(pl.multiple_of(at * m, LANES), m)] = mixed[j][:, 0:m]
        line[:, pl.ds(pl.multiple_of(at * nl, LANES), nl)] = mixed[j][:, m:]
    for j in range(wake_count):
        at = lax.rem(w + wake_count - j, wake_count)
        plane[:, pl.ds(pl.multiple_of(at * nl, LANES), nl)] = planes[j][...]
    count = plane.shape[1]
    targets = panels.shape[1]
    px, py, pz = (plane[k : k + 1, :] for k in range(3))
    sx, sy, sz = (plane[k : k + 1, :] for k in range(3, 6))
    blank = jnp.zeros((2, count), jnp.float32)
    source = jnp.concatenate(
        [sx, sy, sz, py * sz - pz * sy, pz * sx - px * sz, px * sy - py * sx, blank], axis=0
    )
    high, middle, low = thirds(source)
    left[...] = jnp.concatenate([high, high, middle, high, low, middle], axis=0).T.astype(
        jnp.bfloat16
    )
    cx, cy, cz = (panels[k : k + 1, :] for k in range(3))
    nx, ny, nz = (panels[k : k + 1, :] for k in range(4, 7))
    blank = jnp.zeros((2, targets), jnp.float32)
    target = jnp.concatenate(
        [ny * cz - nz * cy, nz * cx - nx * cz, nx * cy - ny * cx, -nx, -ny, -nz, blank], axis=0
    )
    high, middle, low = thirds(target)
    right[...] = jnp.concatenate([high, middle, high, low, high, middle], axis=0).astype(
        jnp.bfloat16
    )
    for tile in range(count // LANES):
        turned = plane[:, tile * LANES : (tile + 1) * LANES].T
        for k in range(3):
            spots[k, tile * LANES : (tile + 1) * LANES, :] = jnp.broadcast_to(
                turned[:, k : k + 1], (LANES, LANES)
            )
        spots[3, tile * LANES : (tile + 1) * LANES, :] = jnp.broadcast_to(
            turned[:, 6:7] * turned[:, 6:7], (LANES, LANES)
        )
    wide = product.shape[2]
    deep = product.shape[1]
    steps = count // deep
    total = targets // wide * steps

    def multiply(step, slot):
        column = lax.div(step, steps)
        block = lax.rem(step, steps)
        product[slot] = jnp.dot(
            left[pl.ds(pl.multiple_of(block * deep, deep), deep), :],
            right[:, pl.ds(pl.multiple_of(column * wide, wide), wide)],
            preferred_element_type=jnp.float32,
        )

    running[...] = jnp.zeros_like(running)
    multiply(0, 0)

    @pl.loop(0, total)
    def _(step):
        slot = lax.rem(step, 2)
        column = lax.div(step, steps)
        block = lax.rem(step, steps)
        multiply(jnp.minimum(step + 1, total - 1), 1 - slot)
        tiles = wide // LANES
        spot = []
        for t in range(tiles):
            lanes = pl.ds(pl.multiple_of(column * wide + t * LANES, LANES), LANES)
            spot.append(
                tuple(jnp.broadcast_to(panels[k : k + 1, lanes], (8, LANES)) for k in range(3))
            )
        sums = [jnp.zeros((8, LANES), jnp.float32)] * tiles
        for g in range(deep // 8):
            at = pl.ds(pl.multiple_of(block * deep + g * 8, 8), 8)
            qx, qy, qz, core = (spots[k, at, :] for k in range(4))
            for t in range(tiles):
                dx = spot[t][0] - qx
                dy = spot[t][1] - qy
                dz = spot[t][2] - qz
                inverse = lax.rsqrt(dx * dx + dy * dy + (dz * dz + core))
                falloff = inverse * inverse * inverse
                sums[t] = sums[t] + falloff * product[
                    slot, g * 8 : g * 8 + 8, t * LANES : (t + 1) * LANES
                ]
        for t in range(tiles):
            running[column * tiles + t] += sums[t]

    @pl.loop(0, targets // LANES)
    def _(tile):
        partial_out[pl.ds(tile, 1), :] = inv_four_pi * jnp.sum(running[tile], axis=0, keepdims=True)

    for tile in range(m // LANES):
        partial_out[pl.ds(p * (m // LANES) + tile, 1), :] += mixed[0][
            7:8, tile * LANES : (tile + 1) * LANES
        ]
    copy.wait()


def pair_kernel(row, rows, plane, line, influence, held, out, keep, turned, sem):
    del held
    copy = pltpu.make_async_copy(
        influence.at[pl.ds(row, rows)], keep.at[pl.ds(row, rows)], sem
    )
    copy.start()
    targets = plane.shape[1]
    sources = line.shape[1]
    for tile in range(sources // LANES):
        turned[tile * LANES : (tile + 1) * LANES, :] = line[
            :, tile * LANES : (tile + 1) * LANES
        ].T
    wide = 2

    @pl.loop(0, targets // (wide * LANES))
    def _(column):
        mine = []
        for t in range(wide):
            lanes = pl.ds(pl.multiple_of((column * wide + t) * LANES, LANES), LANES)
            mine.append([jnp.broadcast_to(plane[k : k + 1, lanes], (8, LANES)) for k in range(7)])
            mine[t][6] = 0.5 * (mine[t][6] * mine[t][6])

        def group(g, sums):
            rows = turned[pl.ds(pl.multiple_of(g * 8, 8), 8), :]
            sums = list(sums)
            other = [jnp.broadcast_to(rows[:, k : k + 1], (8, LANES)) for k in range(7)]
            half = 0.5 * (other[6] * other[6])
            for t in range(wide):
                tx, ty, tz, ux, uy, uz, core = mine[t]
                ox, oy, oz, sx, sy, sz, _ = other
                dx, dy, dz = tx - ox, ty - oy, tz - oz
                inverse = lax.rsqrt(dx * dx + dy * dy + dz * dz + (core + half))
                square = inverse * inverse
                falloff = square * inverse
                crosses = (dy * sz - dz * sy, dz * sx - dx * sz, dx * sy - dy * sx)
                twists = (uy * sz - uz * sy, uz * sx - ux * sz, ux * sy - uy * sx)
                along = 3.0 * square * (ux * dx + uy * dy + uz * dz)
                for k in range(3):
                    sums[6 * t + k] += falloff * crosses[k]
                    sums[6 * t + 3 + k] += falloff * (twists[k] - along * crosses[k])
            return tuple(sums)

        zero = jnp.zeros((8, LANES), jnp.float32)
        sums = lax.fori_loop(0, sources // 8, group, (zero,) * (6 * wide), unroll=4)
        for t in range(wide):
            lanes = pl.ds(pl.multiple_of((column * wide + t) * LANES, LANES), LANES)
            for k in range(6):
                out[k : k + 1, lanes] = jnp.sum(sums[6 * t + k], axis=0, keepdims=True)
            out[6:8, lanes] = jnp.zeros((2, LANES), jnp.float32)

    copy.wait()


def product_kernel(opening, wake_count, panel_count, fresh, streamed, *refs):
    refs = list(refs)
    take = lambda count: [refs.pop(0) for _ in range(count)]
    blocks = take(wake_count)
    keep, influence = take(2)
    if opening:
        out, side, keep = take(3)
    else:
        side, out = take(2)
    column, flat, sums, ring, sem = take(5)
    first, rows = streamed
    chunks = rows // RING_ROWS
    extra = fresh[1] // RING_ROWS if opening else 0
    kept = (fresh[0] if opening else first) // RING_ROWS

    def fetch(i):
        return pltpu.make_async_copy(
            influence.at[pl.ds(first + i * RING_ROWS, RING_ROWS)],
            ring.at[i % RING],
            sem.at[i % RING],
        )

    def settle(i):
        return pltpu.make_async_copy(
            influence.at[pl.ds(fresh[0] + i * RING_ROWS, RING_ROWS)],
            keep.at[pl.ds(fresh[0] + i * RING_ROWS, RING_ROWS)],
            sem.at[RING + i],
        )

    for i in range(extra):
        settle(i).start()
    for i in range(min(RING, chunks)):
        fetch(i).start()
    w = lax.axis_index("wake")
    p = lax.axis_index("panel")
    ways = wake_count // panel_count
    height = blocks[0].shape[0]
    for e in range(ways):
        value = None
        for j in range(wake_count):
            term = blocks[j][...]
            if ways > 1:
                sender = lax.rem(w + wake_count - j, wake_count)
                term = jnp.where(sender // panel_count == e, term, 0.0)
            value = term if value is None else value + term
        if opening:
            side[e * height : (e + 1) * height, :] = value
            value = relax_factor * value
        flat[e * height : (e + 1) * height, :] = value
        for k in range(height):
            column[e * height + k] = jnp.broadcast_to(value[k : k + 1, :], (8, LANES))
    tiles = column.shape[0]
    vectors = [column[k] for k in range(tiles)]

    def block(ref, start, at, height):
        for g in range(height // 8):
            even = odd = None
            for k in range(0, tiles, 2):
                a = ref[pl.ds(start + 8 * g, 8), k * LANES : (k + 1) * LANES] * vectors[k]
                b = ref[pl.ds(start + 8 * g, 8), (k + 1) * LANES : (k + 2) * LANES] * vectors[k + 1]
                even = a if even is None else even + a
                odd = b if odd is None else odd + b
            sums[pl.ds(at + 8 * g, 8), :] = even + odd

    def kept_blocks(low, high):
        if high > low:

            @pl.loop(low, high)
            def _(i):
                at = pl.multiple_of(i * RING_ROWS, RING_ROWS)
                block(keep, at, at, RING_ROWS)

    low = 0
    for i in range(extra):
        high = kept * (i + 1) // (extra + chunks + 1)
        kept_blocks(low, high)
        low = high
        settle(i).wait()
        block(keep, fresh[0] + i * RING_ROWS, fresh[0] + i * RING_ROWS, RING_ROWS)
    for i in range(chunks):
        high = kept * (extra + i + 1) // (extra + chunks + 1)
        kept_blocks(low, high)
        low = high
        fetch(i).wait()
        block(ring.at[i % RING], 0, first + i * RING_ROWS, RING_ROWS)
        if i + RING < chunks:
            fetch(i + RING).start()
    kept_blocks(low, kept)
    lane = lax.broadcasted_iota(jnp.int32, (8, LANES), 1)
    diagonal = (lane & 7) == lax.broadcasted_iota(jnp.int32, (8, LANES), 0)

    @pl.loop(0, out.shape[0], unroll=4)
    def _(i):
        gathered = jnp.zeros((8, LANES), jnp.float32)
        for g in range(LANES // 8):
            part = sums[pl.ds(pl.multiple_of(i * LANES + 8 * g, 8), 8), :]
            gathered = jnp.where((lane >> 3) == g, jnp.sum(part, axis=1, keepdims=True), gathered)
        out[pl.ds(i, 1), :] = -relax_factor * jnp.sum(
            jnp.where(diagonal, gathered, 0.0), axis=0, keepdims=True
        )

    @pl.when(w // ways == p)
    def _():
        own = pl.ds(lax.rem(w, ways) * height, height)
        out[...] += flat[own, :] + relax_factor * side[own, :]


def panel_kernel(wake_count, panel_count, *refs):
    blocks = refs[:panel_count]
    panels, plane, pairs = refs[panel_count : panel_count + 3]
    own_out = refs[panel_count + 3]
    outs = refs[panel_count + 4 : panel_count + 4 + wake_count]
    strengths, results = refs[panel_count + 4 + wake_count :]
    w = lax.axis_index("wake")
    p = lax.axis_index("panel")
    value = blocks[0][...]
    for block in blocks[1:]:
        value = value + block[...]
    strengths[...] = value
    own = own_out.shape[0]
    own_out[...] = strengths[pl.ds(pl.multiple_of(p * own, own), own), :]
    tiles = strengths.shape[0]
    targets = plane.shape[1]
    wide = 4 if targets % (4 * LANES) == 0 else 1
    zero = jnp.zeros((8, LANES), jnp.float32)
    for column in range(targets // (wide * LANES)):
        spot = []
        for t in range(wide):
            start = (column * wide + t) * LANES
            spot.append(
                [
                    jnp.broadcast_to(plane[k : k + 1, start : start + LANES], (8, LANES))
                    for k in range(3)
                ]
            )

        def visit(tile, sums):
            sums = list(sums)
            lanes = pl.ds(pl.multiple_of(tile * LANES, LANES), LANES)
            area = panels[3:4, lanes]
            rows = jnp.concatenate(
                [
                    panels[0:3, lanes],
                    4.0 * area,
                    area * strengths[pl.ds(tile, 1), :],
                    jnp.zeros((3, LANES), jnp.float32),
                ],
                axis=0,
            ).T
            for g in range(LANES // 8):
                cx, cy, cz, size, weight = (
                    jnp.broadcast_to(rows[8 * g : 8 * g + 8, k : k + 1], (8, LANES))
                    for k in range(5)
                )
                for t in range(wide):
                    dx = spot[t][0] - cx
                    dy = spot[t][1] - cy
                    dz = spot[t][2] - cz
                    inverse = lax.rsqrt(dx * dx + dy * dy + (dz * dz + size))
                    weighted = weight * inverse * (inverse * inverse)
                    sums[3 * t] += weighted * dx
                    sums[3 * t + 1] += weighted * dy
                    sums[3 * t + 2] += weighted * dz
            return tuple(sums)

        sums = lax.fori_loop(0, tiles, visit, (zero,) * (3 * wide))
        for t in range(wide):
            start = (column * wide + t) * LANES
            for k in range(3):
                results[k : k + 1, start : start + LANES] = inv_four_pi * (
                    jnp.sum(sums[3 * t + k], axis=0, keepdims=True)
                    - pairs[k : k + 1, start : start + LANES]
                )
    results[3:6, :] = -inv_four_pi * pairs[3:6, :]
    results[6:8, :] = jnp.zeros_like(pairs[6:8, :])
    nl = outs[0].shape[1]
    for j in range(wake_count):
        at = lax.rem(w + j, wake_count)
        outs[j][...] = results[:, pl.ds(pl.multiple_of(at * nl, LANES), nl)]


def final_kernel(count, *refs):
    parts, (velocity, stretching) = refs[:count], refs[count:]
    total = parts[0][...]
    for part in parts[1:]:
        total = total + part[...]
    for axis in range(3):
        velocity[axis : axis + 1, :] = total[axis : axis + 1, :] + freestream[axis]
    stretching[...] = total[3:6, :]


def block_device(
    positions,
    strengths,
    cores,
    panel_centers,
    panel_normals,
    panel_areas,
    influence,
    blade_ids,
    blade_velocity,
):
    wake_count = lax.axis_size("wake")
    panel_count = lax.axis_size("panel")
    ways = wake_count // panel_count
    nl = positions.shape[1]
    m = panel_centers.shape[1]
    rows, columns = influence.shape
    tiles = rows // LANES
    row_bytes = 4 * columns
    most = min(rows, KEEP_BYTES // row_bytes // LANES * LANES)
    counts = [most * share * MIB // KEEP_BYTES // RING_ROWS * RING_ROWS for share in SHARES]
    parts = ((0, counts[0]), (counts[0], counts[1]), (sum(counts), most - sum(counts)))
    streamed = (most, rows - most)
    hold = pltpu.VMEM((most, columns), jnp.float32)
    stay = lambda value: pltpu.with_memory_space_constraint(value, pltpu.VMEM)
    route = functools.partial(send, wake_count=wake_count, panel_count=panel_count)

    particle, mixed = pl.pallas_call(
        pack_kernel,
        out_shape=(f32(8, nl), f32(8, m + nl)),
        in_specs=[hbm] * 8,
        out_specs=(vmem, vmem),
        scratch_shapes=[
            pltpu.VMEM((3, nl), jnp.float32),
            pltpu.VMEM((3, nl), jnp.float32),
            pltpu.VMEM((1, nl), jnp.float32),
            pltpu.VMEM((3, m), jnp.float32),
            pltpu.VMEM((3, m), jnp.float32),
            pltpu.VMEM((1, m), jnp.float32),
            pltpu.VMEM((1, m), jnp.int32),
            pltpu.SMEM(blade_velocity.shape, jnp.float32),
            pltpu.SemaphoreType.DMA((8,)),
        ],
        compiler_params=params(2),
    )(
        *(
            pltpu.with_memory_space_constraint(value, pltpu.HBM)
            for value in (
                positions,
                strengths,
                cores,
                panel_centers,
                panel_normals,
                panel_areas,
                blade_ids[None, :],
                blade_velocity,
            )
        )
    )
    lines = [mixed] + [
        route(mixed, route=lambda w, p, j=j: (w, (p + j) % panel_count))
        for j in range(1, panel_count)
    ]
    planes = [particle] + [
        route(particle, route=lambda w, p, j=j: ((w + j) % wake_count, p))
        for j in range(1, wake_count)
    ]
    deep = math.gcd(wake_count * nl, 512)
    wide = 2 * LANES if rows % (2 * LANES) == 0 else LANES
    panels, plane, line, partial, keep = pl.pallas_call(
        functools.partial(wake_kernel, wake_count, panel_count, *parts[0]),
        out_shape=(
            f32(8, rows),
            f32(8, wake_count * nl),
            f32(8, panel_count * nl),
            f32(tiles, LANES),
            hold,
        ),
        in_specs=[vmem] * (panel_count + wake_count) + [hbm],
        out_specs=(vmem,) * 5,
        scratch_shapes=[
            pltpu.VMEM((wake_count * nl, 48), jnp.bfloat16),
            pltpu.VMEM((48, rows), jnp.bfloat16),
            pltpu.VMEM((2, deep, wide), jnp.float32),
            pltpu.VMEM((4, wake_count * nl, LANES), jnp.float32),
            pltpu.VMEM((tiles, 8, LANES), jnp.float32),
            pltpu.SemaphoreType.DMA,
        ],
        compiler_params=params(max(SCOPED, 4 + wake_count * nl // 512)),
    )(*lines, *planes, influence)

    def exchange(value):
        return [
            route(
                value,
                route=lambda w, p, j=j: (
                    (w % ways * panel_count + p + j) % wake_count,
                    w // ways,
                ),
            )
            for j in range(wake_count)
        ]

    def multiply(blocks, keep, side=None):
        opening = side is None
        outs = [f32(tiles, LANES)]
        if opening:
            outs += [f32(columns // LANES, LANES), hold]
        return pl.pallas_call(
            functools.partial(
                product_kernel, opening, wake_count, panel_count, parts[2], streamed
            ),
            out_shape=outs,
            in_specs=[vmem] * (wake_count + 1) + [hbm] + [vmem] * (not opening),
            out_specs=[vmem] * len(outs),
            input_output_aliases={wake_count: 2} if opening else {},
            scratch_shapes=[
                pltpu.VMEM((columns // LANES, 8, LANES), jnp.float32),
                pltpu.VMEM((columns // LANES, LANES), jnp.float32),
                pltpu.VMEM((rows, LANES), jnp.float32),
                pltpu.VMEM((RING, RING_ROWS, columns), jnp.float32),
                pltpu.SemaphoreType.DMA((RING + parts[2][1] // RING_ROWS,)),
            ],
            compiler_params=params(SCOPED),
        )(*blocks, stay(keep), influence, *([] if opening else [side]))

    blocks = exchange(partial)
    pairs, keep = pl.pallas_call(
        functools.partial(pair_kernel, *parts[1]),
        out_shape=(f32(8, wake_count * nl), hold),
        in_specs=[vmem, vmem, hbm, vmem],
        out_specs=(vmem, vmem),
        input_output_aliases={3: 1},
        scratch_shapes=[
            pltpu.VMEM((panel_count * nl, 8), jnp.float32),
            pltpu.SemaphoreType.DMA,
        ],
        compiler_params=params(SCOPED),
    )(plane, line, influence, stay(keep))
    partial, right_side, keep = multiply(blocks, keep)
    for turn in range(ITERS - 2):
        (partial,) = multiply(exchange(partial), keep, right_side)
    ends = [partial] + [
        route(partial, route=lambda w, p, j=j: (w, (p + j) % panel_count))
        for j in range(1, panel_count)
    ]
    own, *sums = pl.pallas_call(
        functools.partial(panel_kernel, wake_count, panel_count),
        out_shape=(f32(m // LANES, LANES),) + (f32(8, nl),) * wake_count,
        in_specs=[vmem] * (panel_count + 3),
        out_specs=(vmem,) * (1 + wake_count),
        scratch_shapes=[
            pltpu.VMEM((tiles, LANES), jnp.float32),
            pltpu.VMEM((8, wake_count * nl), jnp.float32),
        ],
        compiler_params=params(2),
    )(*ends, panels, plane, pairs)
    received = [sums[0]] + [
        route(sums[j], route=lambda w, p, j=j: ((w + j) % wake_count, p))
        for j in range(1, wake_count)
    ]
    velocity, stretching = pl.pallas_call(
        functools.partial(final_kernel, wake_count),
        out_shape=(f32(3, nl), f32(3, nl)),
        in_specs=[vmem] * wake_count,
        out_specs=(vmem, vmem),
        compiler_params=params(1),
    )(*received)
    return (velocity, stretching, own.reshape(m))


def fits(positions, panel_centers, influence):
    wake_count = lax.axis_size("wake")
    panel_count = lax.axis_size("panel")
    return (
        wake_count % panel_count == 0
        and positions.shape[1] % LANES == 0
        and wake_count * positions.shape[1] % (2 * LANES) == 0
        and panel_centers.shape[1] % LANES == 0
        and influence.shape[1] % (2 * LANES) == 0
    )


def per_device(*arrays):
    if fits(arrays[0], arrays[3], arrays[6]):
        return block_device(*arrays)
    return plain_device(*arrays)


def solution(mesh):
    in_specs = (
        P(None, ("groups", "wake", "panel")),
        P(None, ("groups", "wake", "panel")),
        P(None, ("groups", "wake", "panel")),
        P(None, ("groups", "wake", "panel")),
        P(None, ("groups", "wake", "panel")),
        P(None, ("groups", "wake", "panel")),
        P(("groups", "wake"), "panel"),
        P(("groups", "wake", "panel")),
        P("groups", None),
    )
    out_specs = (
        P(None, ("groups", "wake", "panel")),
        P(None, ("groups", "wake", "panel")),
        P(("groups", "wake", "panel")),
    )
    return jax.shard_map(
        per_device, mesh=mesh, in_specs=in_specs, out_specs=out_specs, check_vma=False
    )
```

```python
import functools
import math

import jax
import jax.numpy as jnp
from jax import lax
from jax.experimental import pallas as pl
from jax.experimental.pallas import tpu as pltpu
from jax.sharding import PartitionSpec as P

BLADES = 4
ITERS = 4


inv_four_pi = 1.0 / (4.0 * math.pi)
relax_factor = 0.5
freestream = (0.0, 0.0, -1.0)
block_width = 2048


def spread(block, axis, source):
    block = jnp.where(lax.axis_index(axis) == source, block, jnp.zeros_like(block))
    return lax.psum(block, axis)


def vortex_terms(targets, sources):
    target_pos, target_str, target_core = targets
    source_pos, source_str, source_core = sources
    offset_x = target_pos[0][:, None] - source_pos[0][None, :]
    offset_y = target_pos[1][:, None] - source_pos[1][None, :]
    offset_z = target_pos[2][:, None] - source_pos[2][None, :]
    core_sq = 0.5 * (
        target_core[0][:, None] * target_core[0][:, None]
        + source_core[0][None, :] * source_core[0][None, :]
    )
    distance = offset_x * offset_x + offset_y * offset_y + offset_z * offset_z + core_sq
    inverse = lax.rsqrt(distance)
    falloff = inverse * inverse * inverse
    steeper = falloff * inverse * inverse
    source_x = source_str[0][None, :]
    source_y = source_str[1][None, :]
    source_z = source_str[2][None, :]
    target_x = target_str[0][:, None]
    target_y = target_str[1][:, None]
    target_z = target_str[2][:, None]
    cross_x = offset_y * source_z - offset_z * source_y
    cross_y = offset_z * source_x - offset_x * source_z
    cross_z = offset_x * source_y - offset_y * source_x
    twist_x = target_y * source_z - target_z * source_y
    twist_y = target_z * source_x - target_x * source_z
    twist_z = target_x * source_y - target_y * source_x
    along = 3.0 * steeper * (target_x * offset_x + target_y * offset_y + target_z * offset_z)
    return jnp.stack(
        [
            jnp.sum(falloff * cross_x, axis=1),
            jnp.sum(falloff * cross_y, axis=1),
            jnp.sum(falloff * cross_z, axis=1),
            jnp.sum(falloff * twist_x - along * cross_x, axis=1),
            jnp.sum(falloff * twist_y - along * cross_y, axis=1),
            jnp.sum(falloff * twist_z - along * cross_z, axis=1),
        ]
    )


def wake_terms(targets, sources):
    points = targets[0]
    source_pos, source_str, source_core = sources
    offset_x = points[0][:, None] - source_pos[0][None, :]
    offset_y = points[1][:, None] - source_pos[1][None, :]
    offset_z = points[2][:, None] - source_pos[2][None, :]
    distance = (
        offset_x * offset_x
        + offset_y * offset_y
        + offset_z * offset_z
        + source_core[0][None, :] * source_core[0][None, :]
    )
    inverse = lax.rsqrt(distance)
    falloff = inverse * inverse * inverse
    source_x = source_str[0][None, :]
    source_y = source_str[1][None, :]
    source_z = source_str[2][None, :]
    return jnp.stack(
        [
            jnp.sum(falloff * (offset_y * source_z - offset_z * source_y), axis=1),
            jnp.sum(falloff * (offset_z * source_x - offset_x * source_z), axis=1),
            jnp.sum(falloff * (offset_x * source_y - offset_y * source_x), axis=1),
        ]
    )


def panel_terms(targets, sources):
    points = targets[0]
    centers, weights, areas = sources
    offset_x = points[0][:, None] - centers[0][None, :]
    offset_y = points[1][:, None] - centers[1][None, :]
    offset_z = points[2][:, None] - centers[2][None, :]
    distance = (
        offset_x * offset_x + offset_y * offset_y + offset_z * offset_z + 4.0 * areas[0][None, :]
    )
    inverse = lax.rsqrt(distance)
    weighted = weights[0][None, :] * inverse * inverse * inverse
    return jnp.stack(
        [
            jnp.sum(weighted * offset_x, axis=1),
            jnp.sum(weighted * offset_y, axis=1),
            jnp.sum(weighted * offset_z, axis=1),
        ]
    )


def over_sources(kernel, targets, sources, width, out_rows):
    length = sources[0].shape[-1]
    stride = math.gcd(length, width)
    if stride == length:
        return kernel(targets, sources)
    pieces = tuple(
        (
            jnp.moveaxis(source.reshape(source.shape[0], length // stride, stride), 1, 0)
            for source in sources
        )
    )

    def visit(running, entry):
        return (running + kernel(targets, entry), None)

    initial = jnp.zeros((out_rows, targets[0].shape[-1]), jnp.float32)
    running, unused = lax.scan(visit, initial, pieces)
    return running


def column_of(row_block):
    wake_count = lax.axis_size("wake")
    panel_count = lax.axis_size("panel")
    panel_at = lax.axis_index("panel")
    first_root = panel_at * wake_count // panel_count
    donors = max(1, wake_count // panel_count)
    pieces = []
    for offset_rank in range(donors):
        pieces.append(spread(row_block, "wake", first_root + offset_rank))
    joined = pieces[0] if donors == 1 else jnp.concatenate(pieces, axis=0)
    return joined


def relax(right_side, influence):
    row_side = lax.all_gather(right_side, "panel", axis=0, tiled=True)
    current = relax_factor * row_side
    for turn in range(ITERS - 1):
        column = column_of(current)
        partial_value = jnp.dot(influence, column, precision=lax.Precision.HIGHEST)
        image = lax.psum(partial_value, "panel")
        current = current + relax_factor * (row_side - image)
    own_start = lax.axis_index("panel") * right_side.shape[0]
    return lax.dynamic_slice_in_dim(current, own_start, right_side.shape[0], 0)


def plain_device(
    positions,
    strengths,
    cores,
    panel_centers,
    panel_normals,
    panel_areas,
    influence,
    blade_ids,
    blade_velocity,
):
    onset_dir = jnp.asarray(freestream, jnp.float32)[:, None]
    onehot = (blade_ids[None, :] == jnp.arange(BLADES, dtype=jnp.int32)[:, None]).astype(
        jnp.float32
    )
    kinematic = jnp.dot(blade_velocity.T, onehot, precision=lax.Precision.HIGHEST) + onset_dir
    moving = -jnp.sum(panel_normals * kinematic, axis=0)
    particles = (positions, strengths, cores)
    piece = (
        lax.all_gather(positions, ("wake", "panel"), axis=1, tiled=True),
        lax.all_gather(strengths, ("wake", "panel"), axis=1, tiled=True),
        lax.all_gather(cores, ("wake", "panel"), axis=1, tiled=True),
    )
    pair_sums = over_sources(vortex_terms, particles, piece, block_width, 6)
    wake_sums = over_sources(wake_terms, (panel_centers,), piece, block_width, 3)
    right_side = moving + inv_four_pi * jnp.sum(panel_normals * wake_sums, axis=0)
    centers, areas = (
        lax.all_gather(panel_centers, ("wake", "panel"), axis=1, tiled=True),
        lax.all_gather(panel_areas, ("wake", "panel"), axis=1, tiled=True),
    )
    panel_strengths = relax(right_side, influence)
    all_strengths = lax.all_gather(panel_strengths, ("wake", "panel"), axis=0, tiled=True)
    weights = (all_strengths * areas[0])[None, :]
    panel_sums = over_sources(panel_terms, (positions,), (centers, weights, areas), block_width, 3)
    velocity = onset_dir - inv_four_pi * pair_sums[:3] + inv_four_pi * panel_sums
    stretching = -inv_four_pi * pair_sums[3:]
    return (velocity, stretching, panel_strengths)


LANES = 128
MIB = 1 << 20
KEEP_BYTES = 50 * MIB
SHARES = (25, 13)
SCOPED = 7
RING_ROWS = 64
RING = 4
AXES = ("wake", "panel")

vmem = pl.BlockSpec(memory_space=pltpu.VMEM)
hbm = pl.BlockSpec(memory_space=pltpu.HBM)


def f32(*shape):
    return jax.ShapeDtypeStruct(shape, jnp.float32)


def near(*shape):
    return pltpu.VMEM(shape, jnp.float32)


def stay(*values):
    return tuple(pltpu.with_memory_space_constraint(value, pltpu.VMEM) for value in values)


def params(mib):
    return pltpu.CompilerParams(vmem_limit_bytes=mib * MIB)


def send(value, wake_count, panel_count, route):
    pairs = []
    for w in range(wake_count):
        for p in range(panel_count):
            target = route(w, p)
            if target is not None:
                pairs.append((w * panel_count + p, target[0] * panel_count + target[1]))
    return lax.ppermute(value, AXES, pairs)


def pack_kernel(*refs):
    sources, (particle_out, mixed_out), held, sems = refs[:8], refs[8:10], refs[10:18], refs[18]
    copies = [
        pltpu.make_async_copy(source, target, sems.at[i])
        for i, (source, target) in enumerate(zip(sources, held))
    ]
    for copy in copies:
        copy.start()
    for copy in copies:
        copy.wait()
    positions, strengths, cores, centers, normals, areas, ids, blades = held
    particle_out[0:3, :] = positions[...]
    particle_out[3:6, :] = strengths[...]
    particle_out[6:7, :] = cores[...]
    particle_out[7:8, :] = jnp.zeros_like(cores[...])
    width = centers.shape[1]
    mixed_out[0:3, 0:width] = centers[...]
    mixed_out[3:4, 0:width] = areas[...]
    mixed_out[4:7, 0:width] = normals[...]
    owner = ids[...]
    total = None
    for axis in range(3):
        speed = jnp.zeros(owner.shape, jnp.float32)
        for blade in range(BLADES):
            speed = jnp.where(owner == blade, blades[blade, axis], speed)
        term = normals[axis : axis + 1, :] * (speed + freestream[axis])
        total = term if total is None else total + term
    mixed_out[7:8, 0:width] = -total
    mixed_out[:, width:] = particle_out[...]


def thirds(value):
    high = value.astype(jnp.bfloat16).astype(jnp.float32)
    rest = value - high
    middle = rest.astype(jnp.bfloat16).astype(jnp.float32)
    return high, middle, rest - middle


def wake_kernel(wake_count, panel_count, row, rows, *refs):
    mixed = refs[:panel_count]
    planes = refs[panel_count : panel_count + wake_count]
    influence, panels, plane, line, partial_out, keep = refs[panel_count + wake_count :][:6]
    left, right, product, spots, running, sem = refs[panel_count + wake_count + 6 :]
    copy = pltpu.make_async_copy(
        influence.at[pl.ds(row, rows)], keep.at[pl.ds(row, rows)], sem
    )
    copy.start()
    w = lax.axis_index("wake")
    p = lax.axis_index("panel")
    nl = planes[0].shape[1]
    m = mixed[0].shape[1] - nl
    for j in range(panel_count):
        at = lax.rem(p + panel_count - j, panel_count)
        panels[:, pl.ds(pl.multiple_of(at * m, LANES), m)] = mixed[j][:, 0:m]
        line[:, pl.ds(pl.multiple_of(at * nl, LANES), nl)] = mixed[j][:, m:]
    for j in range(wake_count):
        at = lax.rem(w + wake_count - j, wake_count)
        plane[:, pl.ds(pl.multiple_of(at * nl, LANES), nl)] = planes[j][...]
    count = plane.shape[1]
    targets = panels.shape[1]
    px, py, pz = (plane[k : k + 1, :] for k in range(3))
    sx, sy, sz = (plane[k : k + 1, :] for k in range(3, 6))
    blank = jnp.zeros((2, count), jnp.float32)
    source = jnp.concatenate(
        [sx, sy, sz, py * sz - pz * sy, pz * sx - px * sz, px * sy - py * sx, blank], axis=0
    )
    high, middle, low = thirds(source)
    left[...] = jnp.concatenate([high, high, middle, high, low, middle], axis=0).T.astype(
        jnp.bfloat16
    )
    cx, cy, cz = (panels[k : k + 1, :] for k in range(3))
    nx, ny, nz = (panels[k : k + 1, :] for k in range(4, 7))
    blank = jnp.zeros((2, targets), jnp.float32)
    target = jnp.concatenate(
        [ny * cz - nz * cy, nz * cx - nx * cz, nx * cy - ny * cx, -nx, -ny, -nz, blank], axis=0
    )
    high, middle, low = thirds(target)
    right[...] = jnp.concatenate([high, middle, high, low, high, middle], axis=0).astype(
        jnp.bfloat16
    )
    for tile in range(count // LANES):
        turned = plane[:, tile * LANES : (tile + 1) * LANES].T
        for k in range(3):
            spots[k, tile * LANES : (tile + 1) * LANES, :] = jnp.broadcast_to(
                turned[:, k : k + 1], (LANES, LANES)
            )
        spots[3, tile * LANES : (tile + 1) * LANES, :] = jnp.broadcast_to(
            turned[:, 6:7] * turned[:, 6:7], (LANES, LANES)
        )
    wide = product.shape[2]
    deep = product.shape[1]
    steps = count // deep
    total = targets // wide * steps

    def multiply(step, slot):
        column = lax.div(step, steps)
        block = lax.rem(step, steps)
        product[slot] = jnp.dot(
            left[pl.ds(pl.multiple_of(block * deep, deep), deep), :],
            right[:, pl.ds(pl.multiple_of(column * wide, wide), wide)],
            preferred_element_type=jnp.float32,
        )

    running[...] = jnp.zeros_like(running)
    multiply(0, 0)

    @pl.loop(0, total)
    def _(step):
        slot = lax.rem(step, 2)
        column = lax.div(step, steps)
        block = lax.rem(step, steps)
        multiply(jnp.minimum(step + 1, total - 1), 1 - slot)
        tiles = wide // LANES
        spot = []
        for t in range(tiles):
            lanes = pl.ds(pl.multiple_of(column * wide + t * LANES, LANES), LANES)
            spot.append(
                tuple(jnp.broadcast_to(panels[k : k + 1, lanes], (8, LANES)) for k in range(3))
            )
        sums = [jnp.zeros((8, LANES), jnp.float32)] * tiles
        for g in range(deep // 8):
            at = pl.ds(pl.multiple_of(block * deep + g * 8, 8), 8)
            qx, qy, qz, core = (spots[k, at, :] for k in range(4))
            for t in range(tiles):
                dx = spot[t][0] - qx
                dy = spot[t][1] - qy
                dz = spot[t][2] - qz
                inverse = lax.rsqrt(dx * dx + dy * dy + (dz * dz + core))
                falloff = inverse * inverse * inverse
                sums[t] = sums[t] + falloff * product[
                    slot, g * 8 : g * 8 + 8, t * LANES : (t + 1) * LANES
                ]
        for t in range(tiles):
            running[column * tiles + t] += sums[t]

    @pl.loop(0, targets // LANES)
    def _(tile):
        partial_out[pl.ds(tile, 1), :] = inv_four_pi * jnp.sum(running[tile], axis=0, keepdims=True)

    for tile in range(m // LANES):
        partial_out[pl.ds(p * (m // LANES) + tile, 1), :] += mixed[0][
            7:8, tile * LANES : (tile + 1) * LANES
        ]
    copy.wait()


def pair_kernel(row, rows, plane, line, influence, held, out, keep, turned, sem):
    del held
    copy = pltpu.make_async_copy(
        influence.at[pl.ds(row, rows)], keep.at[pl.ds(row, rows)], sem
    )
    copy.start()
    targets = plane.shape[1]
    sources = line.shape[1]
    for tile in range(sources // LANES):
        turned[tile * LANES : (tile + 1) * LANES, :] = line[
            :, tile * LANES : (tile + 1) * LANES
        ].T
    wide = 2

    @pl.loop(0, targets // (wide * LANES))
    def _(column):
        mine = []
        for t in range(wide):
            lanes = pl.ds(pl.multiple_of((column * wide + t) * LANES, LANES), LANES)
            mine.append([jnp.broadcast_to(plane[k : k + 1, lanes], (8, LANES)) for k in range(7)])
            mine[t][6] = 0.5 * (mine[t][6] * mine[t][6])

        def group(g, sums):
            rows = turned[pl.ds(pl.multiple_of(g * 8, 8), 8), :]
            sums = list(sums)
            other = [jnp.broadcast_to(rows[:, k : k + 1], (8, LANES)) for k in range(7)]
            half = 0.5 * (other[6] * other[6])
            for t in range(wide):
                tx, ty, tz, ux, uy, uz, core = mine[t]
                ox, oy, oz, sx, sy, sz, _ = other
                dx, dy, dz = tx - ox, ty - oy, tz - oz
                inverse = lax.rsqrt(dx * dx + dy * dy + dz * dz + (core + half))
                square = inverse * inverse
                falloff = square * inverse
                crosses = (dy * sz - dz * sy, dz * sx - dx * sz, dx * sy - dy * sx)
                twists = (uy * sz - uz * sy, uz * sx - ux * sz, ux * sy - uy * sx)
                along = 3.0 * square * (ux * dx + uy * dy + uz * dz)
                for k in range(3):
                    sums[6 * t + k] += falloff * crosses[k]
                    sums[6 * t + 3 + k] += falloff * (twists[k] - along * crosses[k])
            return tuple(sums)

        zero = jnp.zeros((8, LANES), jnp.float32)
        sums = lax.fori_loop(0, sources // 8, group, (zero,) * (6 * wide), unroll=4)
        for t in range(wide):
            lanes = pl.ds(pl.multiple_of((column * wide + t) * LANES, LANES), LANES)
            for k in range(6):
                out[k : k + 1, lanes] = jnp.sum(sums[6 * t + k], axis=0, keepdims=True)
            out[6:8, lanes] = jnp.zeros((2, LANES), jnp.float32)

    copy.wait()


def product_kernel(opening, wake_count, panel_count, fresh, streamed, *refs):
    refs = list(refs)
    take = lambda count: [refs.pop(0) for _ in range(count)]
    blocks = take(wake_count)
    keep, influence = take(2)
    if opening:
        out, side, keep = take(3)
    else:
        side, out = take(2)
    column, flat, sums, ring, sem = take(5)
    first, rows = streamed
    chunks = rows // RING_ROWS
    extra = fresh[1] // RING_ROWS if opening else 0
    kept = (fresh[0] if opening else first) // RING_ROWS

    def fetch(i):
        return pltpu.make_async_copy(
            influence.at[pl.ds(first + i * RING_ROWS, RING_ROWS)],
            ring.at[i % RING],
            sem.at[i % RING],
        )

    def settle(i):
        return pltpu.make_async_copy(
            influence.at[pl.ds(fresh[0] + i * RING_ROWS, RING_ROWS)],
            keep.at[pl.ds(fresh[0] + i * RING_ROWS, RING_ROWS)],
            sem.at[RING + i],
        )

    for i in range(extra):
        settle(i).start()
    for i in range(min(RING, chunks)):
        fetch(i).start()
    w = lax.axis_index("wake")
    p = lax.axis_index("panel")
    ways = wake_count // panel_count
    height = blocks[0].shape[0]
    for e in range(ways):
        value = None
        for j in range(wake_count):
            term = blocks[j][...]
            if ways > 1:
                sender = lax.rem(w + wake_count - j, wake_count)
                term = jnp.where(sender // panel_count == e, term, 0.0)
            value = term if value is None else value + term
        if opening:
            side[e * height : (e + 1) * height, :] = value
            value = relax_factor * value
        flat[e * height : (e + 1) * height, :] = value
        for k in range(height):
            column[e * height + k] = jnp.broadcast_to(value[k : k + 1, :], (8, LANES))
    tiles = column.shape[0]
    vectors = [column[k] for k in range(tiles)]

    def block(ref, start, at, height):
        for g in range(height // 8):
            even = odd = None
            for k in range(0, tiles, 2):
                a = ref[pl.ds(start + 8 * g, 8), k * LANES : (k + 1) * LANES] * vectors[k]
                b = ref[pl.ds(start + 8 * g, 8), (k + 1) * LANES : (k + 2) * LANES] * vectors[k + 1]
                even = a if even is None else even + a
                odd = b if odd is None else odd + b
            sums[pl.ds(at + 8 * g, 8), :] = even + odd

    def kept_blocks(low, high):
        if high > low:

            @pl.loop(low, high)
            def _(i):
                at = pl.multiple_of(i * RING_ROWS, RING_ROWS)
                block(keep, at, at, RING_ROWS)

    low = 0
    for i in range(extra):
        high = kept * (i + 1) // (extra + chunks + 1)
        kept_blocks(low, high)
        low = high
        settle(i).wait()
        block(keep, fresh[0] + i * RING_ROWS, fresh[0] + i * RING_ROWS, RING_ROWS)
    for i in range(chunks):
        high = kept * (extra + i + 1) // (extra + chunks + 1)
        kept_blocks(low, high)
        low = high
        fetch(i).wait()
        block(ring.at[i % RING], 0, first + i * RING_ROWS, RING_ROWS)
        if i + RING < chunks:
            fetch(i + RING).start()
    kept_blocks(low, kept)
    lane = lax.broadcasted_iota(jnp.int32, (8, LANES), 1)
    diagonal = (lane & 7) == lax.broadcasted_iota(jnp.int32, (8, LANES), 0)

    @pl.loop(0, out.shape[0], unroll=4)
    def _(i):
        gathered = jnp.zeros((8, LANES), jnp.float32)
        for g in range(LANES // 8):
            part = sums[pl.ds(pl.multiple_of(i * LANES + 8 * g, 8), 8), :]
            gathered = jnp.where((lane >> 3) == g, jnp.sum(part, axis=1, keepdims=True), gathered)
        out[pl.ds(i, 1), :] = -relax_factor * jnp.sum(
            jnp.where(diagonal, gathered, 0.0), axis=0, keepdims=True
        )

    @pl.when(w // ways == p)
    def _():
        own = pl.ds(lax.rem(w, ways) * height, height)
        out[...] += flat[own, :] + relax_factor * side[own, :]


def panel_kernel(wake_count, panel_count, *refs):
    blocks = refs[:panel_count]
    panels, plane, pairs = refs[panel_count : panel_count + 3]
    own_out = refs[panel_count + 3]
    outs = refs[panel_count + 4 : panel_count + 4 + wake_count]
    strengths, results = refs[panel_count + 4 + wake_count :]
    w = lax.axis_index("wake")
    p = lax.axis_index("panel")
    value = blocks[0][...]
    for block in blocks[1:]:
        value = value + block[...]
    strengths[...] = value
    own = own_out.shape[0]
    own_out[...] = strengths[pl.ds(pl.multiple_of(p * own, own), own), :]
    tiles = strengths.shape[0]
    targets = plane.shape[1]
    wide = 4 if targets % (4 * LANES) == 0 else 1
    zero = jnp.zeros((8, LANES), jnp.float32)
    for column in range(targets // (wide * LANES)):
        spot = []
        for t in range(wide):
            start = (column * wide + t) * LANES
            spot.append(
                [
                    jnp.broadcast_to(plane[k : k + 1, start : start + LANES], (8, LANES))
                    for k in range(3)
                ]
            )

        def visit(tile, sums):
            sums = list(sums)
            lanes = pl.ds(pl.multiple_of(tile * LANES, LANES), LANES)
            area = panels[3:4, lanes]
            rows = jnp.concatenate(
                [
                    panels[0:3, lanes],
                    4.0 * area,
                    area * strengths[pl.ds(tile, 1), :],
                    jnp.zeros((3, LANES), jnp.float32),
                ],
                axis=0,
            ).T
            for g in range(LANES // 8):
                cx, cy, cz, size, weight = (
                    jnp.broadcast_to(rows[8 * g : 8 * g + 8, k : k + 1], (8, LANES))
                    for k in range(5)
                )
                for t in range(wide):
                    dx = spot[t][0] - cx
                    dy = spot[t][1] - cy
                    dz = spot[t][2] - cz
                    inverse = lax.rsqrt(dx * dx + dy * dy + (dz * dz + size))
                    weighted = weight * inverse * (inverse * inverse)
                    sums[3 * t] += weighted * dx
                    sums[3 * t + 1] += weighted * dy
                    sums[3 * t + 2] += weighted * dz
            return tuple(sums)

        sums = lax.fori_loop(0, tiles, visit, (zero,) * (3 * wide))
        for t in range(wide):
            start = (column * wide + t) * LANES
            for k in range(3):
                results[k : k + 1, start : start + LANES] = inv_four_pi * (
                    jnp.sum(sums[3 * t + k], axis=0, keepdims=True)
                    - pairs[k : k + 1, start : start + LANES]
                )
    results[3:6, :] = -inv_four_pi * pairs[3:6, :]
    results[6:8, :] = jnp.zeros_like(pairs[6:8, :])
    nl = outs[0].shape[1]
    for j in range(wake_count):
        at = lax.rem(w + j, wake_count)
        outs[j][...] = results[:, pl.ds(pl.multiple_of(at * nl, LANES), nl)]


def final_kernel(count, *refs):
    parts, (velocity, stretching) = refs[:count], refs[count:]
    total = parts[0][...]
    for part in parts[1:]:
        total = total + part[...]
    for axis in range(3):
        velocity[axis : axis + 1, :] = total[axis : axis + 1, :] + freestream[axis]
    stretching[...] = total[3:6, :]


def block_device(
    positions,
    strengths,
    cores,
    panel_centers,
    panel_normals,
    panel_areas,
    influence,
    blade_ids,
    blade_velocity,
):
    wake_count = lax.axis_size("wake")
    panel_count = lax.axis_size("panel")
    ways = wake_count // panel_count
    nl = positions.shape[1]
    m = panel_centers.shape[1]
    rows, columns = influence.shape
    tiles = rows // LANES
    row_bytes = 4 * columns
    most = min(rows, KEEP_BYTES // row_bytes // LANES * LANES)
    counts = [most * share * MIB // KEEP_BYTES // RING_ROWS * RING_ROWS for share in SHARES]
    parts = ((0, counts[0]), (counts[0], counts[1]), (sum(counts), most - sum(counts)))
    streamed = (most, rows - most)
    hold = pltpu.VMEM((most, columns), jnp.float32)
    route = functools.partial(send, wake_count=wake_count, panel_count=panel_count)

    particle, mixed = pl.pallas_call(
        pack_kernel,
        out_shape=(f32(8, nl), f32(8, m + nl)),
        in_specs=[hbm] * 8,
        out_specs=(vmem, vmem),
        scratch_shapes=[
            pltpu.VMEM((3, nl), jnp.float32),
            pltpu.VMEM((3, nl), jnp.float32),
            pltpu.VMEM((1, nl), jnp.float32),
            pltpu.VMEM((3, m), jnp.float32),
            pltpu.VMEM((3, m), jnp.float32),
            pltpu.VMEM((1, m), jnp.float32),
            pltpu.VMEM((1, m), jnp.int32),
            pltpu.SMEM(blade_velocity.shape, jnp.float32),
            pltpu.SemaphoreType.DMA((8,)),
        ],
        compiler_params=params(2),
    )(
        *(
            pltpu.with_memory_space_constraint(value, pltpu.HBM)
            for value in (
                positions,
                strengths,
                cores,
                panel_centers,
                panel_normals,
                panel_areas,
                blade_ids[None, :],
                blade_velocity,
            )
        )
    )
    lines = [mixed] + [
        route(mixed, route=lambda w, p, j=j: (w, (p + j) % panel_count))
        for j in range(1, panel_count)
    ]
    planes = [particle] + [
        route(particle, route=lambda w, p, j=j: ((w + j) % wake_count, p))
        for j in range(1, wake_count)
    ]
    deep = math.gcd(wake_count * nl, 512)
    wide = 2 * LANES if rows % (2 * LANES) == 0 else LANES
    panels, plane, line, partial, keep = pl.pallas_call(
        functools.partial(wake_kernel, wake_count, panel_count, *parts[0]),
        out_shape=(
            f32(8, rows),
            f32(8, wake_count * nl),
            f32(8, panel_count * nl),
            f32(tiles, LANES),
            hold,
        ),
        in_specs=[vmem] * (panel_count + wake_count) + [hbm],
        out_specs=(vmem,) * 5,
        scratch_shapes=[
            pltpu.VMEM((wake_count * nl, 48), jnp.bfloat16),
            pltpu.VMEM((48, rows), jnp.bfloat16),
            pltpu.VMEM((2, deep, wide), jnp.float32),
            pltpu.VMEM((4, wake_count * nl, LANES), jnp.float32),
            pltpu.VMEM((tiles, 8, LANES), jnp.float32),
            pltpu.SemaphoreType.DMA,
        ],
        compiler_params=params(max(SCOPED, 4 + wake_count * nl // 512)),
    )(*lines, *planes, influence)

    def exchange(value):
        return [
            route(
                value,
                route=lambda w, p, j=j: (
                    (w % ways * panel_count + p + j) % wake_count,
                    w // ways,
                ),
            )
            for j in range(wake_count)
        ]

    def multiply(blocks, keep, side=None):
        opening = side is None
        outs = [near(tiles, LANES)]
        if opening:
            outs += [near(columns // LANES, LANES), hold]
        return pl.pallas_call(
            functools.partial(
                product_kernel, opening, wake_count, panel_count, parts[2], streamed
            ),
            out_shape=outs,
            in_specs=[vmem] * (wake_count + 1) + [hbm] + [vmem] * (not opening),
            out_specs=[vmem] * len(outs),
            input_output_aliases={wake_count: 2} if opening else {},
            scratch_shapes=[
                pltpu.VMEM((columns // LANES, 8, LANES), jnp.float32),
                pltpu.VMEM((columns // LANES, LANES), jnp.float32),
                pltpu.VMEM((rows, LANES), jnp.float32),
                pltpu.VMEM((RING, RING_ROWS, columns), jnp.float32),
                pltpu.SemaphoreType.DMA((RING + parts[2][1] // RING_ROWS,)),
            ],
            compiler_params=params(SCOPED),
        )(*stay(*blocks, keep), influence, *(() if opening else stay(side)))

    blocks = exchange(partial)
    pairs, keep = pl.pallas_call(
        functools.partial(pair_kernel, *parts[1]),
        out_shape=(f32(8, wake_count * nl), hold),
        in_specs=[vmem, vmem, hbm, vmem],
        out_specs=(vmem, vmem),
        input_output_aliases={3: 1},
        scratch_shapes=[
            pltpu.VMEM((panel_count * nl, 8), jnp.float32),
            pltpu.SemaphoreType.DMA,
        ],
        compiler_params=params(SCOPED),
    )(plane, line, influence, *stay(keep))
    partial, right_side, keep = multiply(blocks, keep)
    for turn in range(ITERS - 2):
        (partial,) = multiply(exchange(partial), keep, right_side)
    ends = [partial] + [
        route(partial, route=lambda w, p, j=j: (w, (p + j) % panel_count))
        for j in range(1, panel_count)
    ]
    own, *sums = pl.pallas_call(
        functools.partial(panel_kernel, wake_count, panel_count),
        out_shape=(f32(m // LANES, LANES),) + (near(8, nl),) * wake_count,
        in_specs=[vmem] * (panel_count + 3),
        out_specs=(vmem,) * (1 + wake_count),
        scratch_shapes=[
            pltpu.VMEM((tiles, LANES), jnp.float32),
            pltpu.VMEM((8, wake_count * nl), jnp.float32),
        ],
        compiler_params=params(2),
    )(*ends, panels, plane, pairs)
    received = [sums[0]] + [
        route(sums[j], route=lambda w, p, j=j: ((w + j) % wake_count, p))
        for j in range(1, wake_count)
    ]
    velocity, stretching = pl.pallas_call(
        functools.partial(final_kernel, wake_count),
        out_shape=(f32(3, nl), f32(3, nl)),
        in_specs=[vmem] * wake_count,
        out_specs=(vmem, vmem),
        compiler_params=params(1),
    )(*stay(*received))
    return (velocity, stretching, own.reshape(m))


def fits(positions, panel_centers, influence):
    wake_count = lax.axis_size("wake")
    panel_count = lax.axis_size("panel")
    return (
        wake_count % panel_count == 0
        and positions.shape[1] % LANES == 0
        and wake_count * positions.shape[1] % (2 * LANES) == 0
        and panel_centers.shape[1] % LANES == 0
        and influence.shape[1] % (2 * LANES) == 0
    )


def per_device(*arrays):
    if fits(arrays[0], arrays[3], arrays[6]):
        return block_device(*arrays)
    return plain_device(*arrays)


def solution(mesh):
    in_specs = (
        P(None, ("groups", "wake", "panel")),
        P(None, ("groups", "wake", "panel")),
        P(None, ("groups", "wake", "panel")),
        P(None, ("groups", "wake", "panel")),
        P(None, ("groups", "wake", "panel")),
        P(None, ("groups", "wake", "panel")),
        P(("groups", "wake"), "panel"),
        P(("groups", "wake", "panel")),
        P("groups", None),
    )
    out_specs = (
        P(None, ("groups", "wake", "panel")),
        P(None, ("groups", "wake", "panel")),
        P(("groups", "wake", "panel")),
    )
    return jax.shard_map(
        per_device, mesh=mesh, in_specs=in_specs, out_specs=out_specs, check_vma=False
    )
```

```python
import functools
import math

import jax
import jax.numpy as jnp
from jax import lax
from jax.experimental import pallas as pl
from jax.experimental.pallas import tpu as pltpu
from jax.sharding import PartitionSpec as P

BLADES = 4
ITERS = 4


inv_four_pi = 1.0 / (4.0 * math.pi)
relax_factor = 0.5
freestream = (0.0, 0.0, -1.0)
block_width = 2048


def spread(block, axis, source):
    block = jnp.where(lax.axis_index(axis) == source, block, jnp.zeros_like(block))
    return lax.psum(block, axis)


def vortex_terms(targets, sources):
    target_pos, target_str, target_core = targets
    source_pos, source_str, source_core = sources
    offset_x = target_pos[0][:, None] - source_pos[0][None, :]
    offset_y = target_pos[1][:, None] - source_pos[1][None, :]
    offset_z = target_pos[2][:, None] - source_pos[2][None, :]
    core_sq = 0.5 * (
        target_core[0][:, None] * target_core[0][:, None]
        + source_core[0][None, :] * source_core[0][None, :]
    )
    distance = offset_x * offset_x + offset_y * offset_y + offset_z * offset_z + core_sq
    inverse = lax.rsqrt(distance)
    falloff = inverse * inverse * inverse
    steeper = falloff * inverse * inverse
    source_x = source_str[0][None, :]
    source_y = source_str[1][None, :]
    source_z = source_str[2][None, :]
    target_x = target_str[0][:, None]
    target_y = target_str[1][:, None]
    target_z = target_str[2][:, None]
    cross_x = offset_y * source_z - offset_z * source_y
    cross_y = offset_z * source_x - offset_x * source_z
    cross_z = offset_x * source_y - offset_y * source_x
    twist_x = target_y * source_z - target_z * source_y
    twist_y = target_z * source_x - target_x * source_z
    twist_z = target_x * source_y - target_y * source_x
    along = 3.0 * steeper * (target_x * offset_x + target_y * offset_y + target_z * offset_z)
    return jnp.stack(
        [
            jnp.sum(falloff * cross_x, axis=1),
            jnp.sum(falloff * cross_y, axis=1),
            jnp.sum(falloff * cross_z, axis=1),
            jnp.sum(falloff * twist_x - along * cross_x, axis=1),
            jnp.sum(falloff * twist_y - along * cross_y, axis=1),
            jnp.sum(falloff * twist_z - along * cross_z, axis=1),
        ]
    )


def wake_terms(targets, sources):
    points = targets[0]
    source_pos, source_str, source_core = sources
    offset_x = points[0][:, None] - source_pos[0][None, :]
    offset_y = points[1][:, None] - source_pos[1][None, :]
    offset_z = points[2][:, None] - source_pos[2][None, :]
    distance = (
        offset_x * offset_x
        + offset_y * offset_y
        + offset_z * offset_z
        + source_core[0][None, :] * source_core[0][None, :]
    )
    inverse = lax.rsqrt(distance)
    falloff = inverse * inverse * inverse
    source_x = source_str[0][None, :]
    source_y = source_str[1][None, :]
    source_z = source_str[2][None, :]
    return jnp.stack(
        [
            jnp.sum(falloff * (offset_y * source_z - offset_z * source_y), axis=1),
            jnp.sum(falloff * (offset_z * source_x - offset_x * source_z), axis=1),
            jnp.sum(falloff * (offset_x * source_y - offset_y * source_x), axis=1),
        ]
    )


def panel_terms(targets, sources):
    points = targets[0]
    centers, weights, areas = sources
    offset_x = points[0][:, None] - centers[0][None, :]
    offset_y = points[1][:, None] - centers[1][None, :]
    offset_z = points[2][:, None] - centers[2][None, :]
    distance = (
        offset_x * offset_x + offset_y * offset_y + offset_z * offset_z + 4.0 * areas[0][None, :]
    )
    inverse = lax.rsqrt(distance)
    weighted = weights[0][None, :] * inverse * inverse * inverse
    return jnp.stack(
        [
            jnp.sum(weighted * offset_x, axis=1),
            jnp.sum(weighted * offset_y, axis=1),
            jnp.sum(weighted * offset_z, axis=1),
        ]
    )


def over_sources(kernel, targets, sources, width, out_rows):
    length = sources[0].shape[-1]
    stride = math.gcd(length, width)
    if stride == length:
        return kernel(targets, sources)
    pieces = tuple(
        (
            jnp.moveaxis(source.reshape(source.shape[0], length // stride, stride), 1, 0)
            for source in sources
        )
    )

    def visit(running, entry):
        return (running + kernel(targets, entry), None)

    initial = jnp.zeros((out_rows, targets[0].shape[-1]), jnp.float32)
    running, unused = lax.scan(visit, initial, pieces)
    return running


def column_of(row_block):
    wake_count = lax.axis_size("wake")
    panel_count = lax.axis_size("panel")
    panel_at = lax.axis_index("panel")
    first_root = panel_at * wake_count // panel_count
    donors = max(1, wake_count // panel_count)
    pieces = []
    for offset_rank in range(donors):
        pieces.append(spread(row_block, "wake", first_root + offset_rank))
    joined = pieces[0] if donors == 1 else jnp.concatenate(pieces, axis=0)
    return joined


def relax(right_side, influence):
    row_side = lax.all_gather(right_side, "panel", axis=0, tiled=True)
    current = relax_factor * row_side
    for turn in range(ITERS - 1):
        column = column_of(current)
        partial_value = jnp.dot(influence, column, precision=lax.Precision.HIGHEST)
        image = lax.psum(partial_value, "panel")
        current = current + relax_factor * (row_side - image)
    own_start = lax.axis_index("panel") * right_side.shape[0]
    return lax.dynamic_slice_in_dim(current, own_start, right_side.shape[0], 0)


def plain_device(
    positions,
    strengths,
    cores,
    panel_centers,
    panel_normals,
    panel_areas,
    influence,
    blade_ids,
    blade_velocity,
):
    onset_dir = jnp.asarray(freestream, jnp.float32)[:, None]
    onehot = (blade_ids[None, :] == jnp.arange(BLADES, dtype=jnp.int32)[:, None]).astype(
        jnp.float32
    )
    kinematic = jnp.dot(blade_velocity.T, onehot, precision=lax.Precision.HIGHEST) + onset_dir
    moving = -jnp.sum(panel_normals * kinematic, axis=0)
    particles = (positions, strengths, cores)
    piece = (
        lax.all_gather(positions, ("wake", "panel"), axis=1, tiled=True),
        lax.all_gather(strengths, ("wake", "panel"), axis=1, tiled=True),
        lax.all_gather(cores, ("wake", "panel"), axis=1, tiled=True),
    )
    pair_sums = over_sources(vortex_terms, particles, piece, block_width, 6)
    wake_sums = over_sources(wake_terms, (panel_centers,), piece, block_width, 3)
    right_side = moving + inv_four_pi * jnp.sum(panel_normals * wake_sums, axis=0)
    centers, areas = (
        lax.all_gather(panel_centers, ("wake", "panel"), axis=1, tiled=True),
        lax.all_gather(panel_areas, ("wake", "panel"), axis=1, tiled=True),
    )
    panel_strengths = relax(right_side, influence)
    all_strengths = lax.all_gather(panel_strengths, ("wake", "panel"), axis=0, tiled=True)
    weights = (all_strengths * areas[0])[None, :]
    panel_sums = over_sources(panel_terms, (positions,), (centers, weights, areas), block_width, 3)
    velocity = onset_dir - inv_four_pi * pair_sums[:3] + inv_four_pi * panel_sums
    stretching = -inv_four_pi * pair_sums[3:]
    return (velocity, stretching, panel_strengths)


LANES = 128
MIB = 1 << 20
KEEP_BYTES = 50 * MIB
SHARES = (7, 21, 13)
SCOPED = 7
RING_ROWS = 64
RING = 4
AXES = ("wake", "panel")

vmem = pl.BlockSpec(memory_space=pltpu.VMEM)
hbm = pl.BlockSpec(memory_space=pltpu.HBM)
anywhere = pl.BlockSpec(memory_space=pl.ANY)


def f32(*shape):
    return jax.ShapeDtypeStruct(shape, jnp.float32)


def near(*shape):
    return pltpu.VMEM(shape, jnp.float32)


def stay(*values):
    return tuple(pltpu.with_memory_space_constraint(value, pltpu.VMEM) for value in values)


def params(mib):
    return pltpu.CompilerParams(vmem_limit_bytes=mib * MIB)


def send(value, wake_count, panel_count, route):
    pairs = []
    for w in range(wake_count):
        for p in range(panel_count):
            target = route(w, p)
            if target is not None:
                pairs.append((w * panel_count + p, target[0] * panel_count + target[1]))
    return lax.ppermute(value, AXES, pairs)


def partner(index, step, count):
    if count & (count - 1) == 0:
        return index ^ step
    return (index + count - step) % count


def pack_kernel(*refs):
    sources, (particle_out, mixed_out), held, sems = refs[:8], refs[8:10], refs[10:18], refs[18]
    copies = [
        pltpu.make_async_copy(source, target, sems.at[i])
        for i, (source, target) in enumerate(zip(sources, held))
    ]
    for copy in copies:
        copy.start()
    for copy in copies:
        copy.wait()
    positions, strengths, cores, centers, normals, areas, ids, blades = held
    particle_out[0:3, :] = positions[...]
    particle_out[3:6, :] = strengths[...]
    particle_out[6:7, :] = cores[...]
    particle_out[7:8, :] = jnp.zeros_like(cores[...])
    width = centers.shape[1]
    mixed_out[0:3, 0:width] = centers[...]
    mixed_out[3:4, 0:width] = areas[...]
    mixed_out[4:7, 0:width] = normals[...]
    owner = ids[...]
    total = None
    for axis in range(3):
        speed = jnp.zeros(owner.shape, jnp.float32)
        for blade in range(BLADES):
            speed = jnp.where(owner == blade, blades[blade, axis], speed)
        term = normals[axis : axis + 1, :] * (speed + freestream[axis])
        total = term if total is None else total + term
    mixed_out[7:8, 0:width] = -total
    mixed_out[:, width:] = particle_out[...]


def load_kernel(row, rows, after, influence, keep, sem):
    del after
    copy = pltpu.make_async_copy(
        influence.at[pl.ds(row, rows)], keep.at[pl.ds(row, rows)], sem
    )
    copy.start()
    copy.wait()


def thirds(value):
    high = value.astype(jnp.bfloat16).astype(jnp.float32)
    rest = value - high
    middle = rest.astype(jnp.bfloat16).astype(jnp.float32)
    return high, middle, rest - middle


def wake_kernel(wake_count, panel_count, row, rows, *refs):
    mixed = refs[:panel_count]
    planes = refs[panel_count : panel_count + wake_count]
    influence, _, panels_out, plane_out, line_out, partial_out, keep = refs[
        panel_count + wake_count :
    ][:7]
    panels, plane, line, left, right, product, spots, running, sem, sems = refs[
        panel_count + wake_count + 7 :
    ]
    w = lax.axis_index("wake")
    p = lax.axis_index("panel")
    nl = planes[0].shape[1]
    m = mixed[0].shape[1] - nl
    moves = []
    for j in range(wake_count):
        at = lax.rem(w + wake_count - j, wake_count)
        moves.append((planes[j], plane.at[:, pl.ds(pl.multiple_of(at * nl, LANES), nl)]))
    for j in range(panel_count):
        at = partner(p, j, panel_count)
        moves.append(
            (mixed[j].at[:, 0:m], panels.at[:, pl.ds(pl.multiple_of(at * m, LANES), m)])
        )
        moves.append(
            (mixed[j].at[:, m : m + nl], line.at[:, pl.ds(pl.multiple_of(at * nl, LANES), nl)])
        )
    moves = [
        pltpu.make_async_copy(source, target, sems.at[i])
        for i, (source, target) in enumerate(moves)
    ]
    for move in moves:
        move.start()
    for move in moves:
        move.wait()
    copy = pltpu.make_async_copy(
        influence.at[pl.ds(row, rows)], keep.at[pl.ds(row, rows)], sem
    )
    results = [
        pltpu.make_async_copy(source, target, sems.at[len(moves) + i])
        for i, (source, target) in enumerate(
            ((panels, panels_out), (plane, plane_out), (line, line_out))
        )
    ]
    for result in results:
        result.start()
    copy.start()
    count = plane.shape[1]
    targets = panels.shape[1]
    px, py, pz = (plane[k : k + 1, :] for k in range(3))
    sx, sy, sz = (plane[k : k + 1, :] for k in range(3, 6))
    blank = jnp.zeros((2, count), jnp.float32)
    source = jnp.concatenate(
        [sx, sy, sz, py * sz - pz * sy, pz * sx - px * sz, px * sy - py * sx, blank], axis=0
    )
    high, middle, low = thirds(source)
    left[...] = jnp.concatenate([high, high, middle, high, low, middle], axis=0).T.astype(
        jnp.bfloat16
    )
    cx, cy, cz = (panels[k : k + 1, :] for k in range(3))
    nx, ny, nz = (panels[k : k + 1, :] for k in range(4, 7))
    blank = jnp.zeros((2, targets), jnp.float32)
    target = jnp.concatenate(
        [ny * cz - nz * cy, nz * cx - nx * cz, nx * cy - ny * cx, -nx, -ny, -nz, blank], axis=0
    )
    high, middle, low = thirds(target)
    right[...] = jnp.concatenate([high, middle, high, low, high, middle], axis=0).astype(
        jnp.bfloat16
    )
    for tile in range(count // LANES):
        turned = plane[:, tile * LANES : (tile + 1) * LANES].T
        for k in range(3):
            spots[k, tile * LANES : (tile + 1) * LANES, :] = jnp.broadcast_to(
                turned[:, k : k + 1], (LANES, LANES)
            )
        spots[3, tile * LANES : (tile + 1) * LANES, :] = jnp.broadcast_to(
            turned[:, 6:7] * turned[:, 6:7], (LANES, LANES)
        )
    wide = product.shape[2]
    deep = product.shape[1]
    steps = count // deep
    total = targets // wide * steps

    def multiply(step, slot):
        column = lax.div(step, steps)
        block = lax.rem(step, steps)
        product[slot] = jnp.dot(
            left[pl.ds(pl.multiple_of(block * deep, deep), deep), :],
            right[:, pl.ds(pl.multiple_of(column * wide, wide), wide)],
            preferred_element_type=jnp.float32,
        )

    running[...] = jnp.zeros_like(running)
    multiply(0, 0)

    @pl.loop(0, total)
    def _(step):
        slot = lax.rem(step, 2)
        column = lax.div(step, steps)
        block = lax.rem(step, steps)
        multiply(jnp.minimum(step + 1, total - 1), 1 - slot)
        tiles = wide // LANES
        spot = []
        for t in range(tiles):
            lanes = pl.ds(pl.multiple_of(column * wide + t * LANES, LANES), LANES)
            spot.append(
                tuple(jnp.broadcast_to(panels[k : k + 1, lanes], (8, LANES)) for k in range(3))
            )
        sums = [jnp.zeros((8, LANES), jnp.float32)] * tiles
        for g in range(deep // 8):
            at = pl.ds(pl.multiple_of(block * deep + g * 8, 8), 8)
            qx, qy, qz, core = (spots[k, at, :] for k in range(4))
            for t in range(tiles):
                dx = spot[t][0] - qx
                dy = spot[t][1] - qy
                dz = spot[t][2] - qz
                inverse = lax.rsqrt(dx * dx + dy * dy + (dz * dz + core))
                falloff = inverse * inverse * inverse
                sums[t] = sums[t] + falloff * product[
                    slot, g * 8 : g * 8 + 8, t * LANES : (t + 1) * LANES
                ]
        for t in range(tiles):
            running[column * tiles + t] += sums[t]

    @pl.loop(0, targets // LANES)
    def _(tile):
        partial_out[pl.ds(tile, 1), :] = inv_four_pi * jnp.sum(running[tile], axis=0, keepdims=True)

    for tile in range(m // LANES):
        partial_out[pl.ds(p * (m // LANES) + tile, 1), :] += panels[
            7:8, pl.ds(pl.multiple_of(p * m + tile * LANES, LANES), LANES)
        ]
    for result in results:
        result.wait()
    copy.wait()


def pair_kernel(
    row, rows, plane_in, line_in, influence, held, out, keep, plane, line, turned, sem, sems
):
    del held
    moves = (
        pltpu.make_async_copy(plane_in, plane, sems.at[0]),
        pltpu.make_async_copy(line_in, line, sems.at[1]),
    )
    for move in moves:
        move.start()
    copy = pltpu.make_async_copy(
        influence.at[pl.ds(row, rows)], keep.at[pl.ds(row, rows)], sem
    )
    copy.start()
    for move in moves:
        move.wait()
    targets = plane.shape[1]
    sources = line.shape[1]
    for tile in range(sources // LANES):
        turned[tile * LANES : (tile + 1) * LANES, :] = line[
            :, tile * LANES : (tile + 1) * LANES
        ].T
    wide = 4 if targets % (4 * LANES) == 0 else 2

    @pl.loop(0, targets // (wide * LANES))
    def _(column):
        mine = []
        for t in range(wide):
            lanes = pl.ds(pl.multiple_of((column * wide + t) * LANES, LANES), LANES)
            mine.append([jnp.broadcast_to(plane[k : k + 1, lanes], (8, LANES)) for k in range(7)])
            mine[t][6] = 0.5 * (mine[t][6] * mine[t][6])

        def group(g, sums):
            rows = turned[pl.ds(pl.multiple_of(g * 8, 8), 8), :]
            sums = list(sums)
            other = [jnp.broadcast_to(rows[:, k : k + 1], (8, LANES)) for k in range(7)]
            half = 0.5 * (other[6] * other[6])
            for t in range(wide):
                tx, ty, tz, ux, uy, uz, core = mine[t]
                ox, oy, oz, sx, sy, sz, _ = other
                dx, dy, dz = tx - ox, ty - oy, tz - oz
                inverse = lax.rsqrt(dx * dx + dy * dy + dz * dz + (core + half))
                square = inverse * inverse
                falloff = square * inverse
                crosses = (dy * sz - dz * sy, dz * sx - dx * sz, dx * sy - dy * sx)
                twists = (uy * sz - uz * sy, uz * sx - ux * sz, ux * sy - uy * sx)
                along = 3.0 * square * (ux * dx + uy * dy + uz * dz)
                for k in range(3):
                    sums[6 * t + k] += falloff * crosses[k]
                    sums[6 * t + 3 + k] += falloff * (twists[k] - along * crosses[k])
            return tuple(sums)

        zero = jnp.zeros((8, LANES), jnp.float32)
        sums = lax.fori_loop(0, sources // 8, group, (zero,) * (6 * wide), unroll=4)
        for t in range(wide):
            lanes = pl.ds(pl.multiple_of((column * wide + t) * LANES, LANES), LANES)
            for k in range(6):
                out[k : k + 1, lanes] = jnp.sum(sums[6 * t + k], axis=0, keepdims=True)
            out[6:8, lanes] = jnp.zeros((2, LANES), jnp.float32)

    copy.wait()


def product_kernel(opening, wake_count, panel_count, fresh, streamed, *refs):
    refs = list(refs)
    take = lambda count: [refs.pop(0) for _ in range(count)]
    blocks = take(wake_count)
    keep, influence = take(2)
    if opening:
        out, side, keep = take(3)
    else:
        side, out = take(2)
    column, flat, sums, ring, sem = take(5)
    first, rows = streamed
    chunks = rows // RING_ROWS
    extra = fresh[1] // RING_ROWS if opening else 0
    kept = (fresh[0] if opening else first) // RING_ROWS

    def fetch(i):
        return pltpu.make_async_copy(
            influence.at[pl.ds(first + i * RING_ROWS, RING_ROWS)],
            ring.at[i % RING],
            sem.at[i % RING],
        )

    def settle(i):
        return pltpu.make_async_copy(
            influence.at[pl.ds(fresh[0] + i * RING_ROWS, RING_ROWS)],
            keep.at[pl.ds(fresh[0] + i * RING_ROWS, RING_ROWS)],
            sem.at[RING + i],
        )

    units = [((i + 0.5) / chunks, fetch, i) for i in range(chunks)]
    units += [((i + 0.5) / extra, settle, i) for i in range(extra)]
    units = [unit[1:] for unit in sorted(units, key=lambda unit: unit[0])]
    ahead = RING + 2 if extra else RING
    if any(
        sum(unit[0] is fetch for unit in units[i : i + ahead]) > RING for i in range(len(units))
    ):
        ahead = RING
    for copy, i in units[:ahead]:
        copy(i).start()
    w = lax.axis_index("wake")
    p = lax.axis_index("panel")
    ways = wake_count // panel_count
    height = blocks[0].shape[0]
    for e in range(ways):
        value = None
        for j in range(wake_count):
            term = blocks[j][...]
            if ways > 1:
                sender = lax.rem(w + wake_count - j, wake_count)
                term = jnp.where(sender // panel_count == e, term, 0.0)
            value = term if value is None else value + term
        if opening:
            side[e * height : (e + 1) * height, :] = value
            value = relax_factor * value
        flat[e * height : (e + 1) * height, :] = value
        for k in range(height):
            column[e * height + k] = jnp.broadcast_to(value[k : k + 1, :], (8, LANES))
    tiles = column.shape[0]
    vectors = [column[k] for k in range(tiles)]

    def block(ref, start, at, height):
        for g in range(height // 8):
            even = odd = None
            for k in range(0, tiles, 2):
                a = ref[pl.ds(start + 8 * g, 8), k * LANES : (k + 1) * LANES] * vectors[k]
                b = ref[pl.ds(start + 8 * g, 8), (k + 1) * LANES : (k + 2) * LANES] * vectors[k + 1]
                even = a if even is None else even + a
                odd = b if odd is None else odd + b
            sums[pl.ds(at + 8 * g, 8), :] = even + odd

    def kept_blocks(low, high):
        if high > low:

            @pl.loop(low, high)
            def _(i):
                at = pl.multiple_of(i * RING_ROWS, RING_ROWS)
                block(keep, at, at, RING_ROWS)

    low = 0
    for n, (copy, i) in enumerate(units):
        high = kept * (n + 1) // (len(units) + 1)
        kept_blocks(low, high)
        low = high
        copy(i).wait()
        if copy is fetch:
            block(ring.at[i % RING], 0, first + i * RING_ROWS, RING_ROWS)
        else:
            at = fresh[0] + i * RING_ROWS
            block(keep, at, at, RING_ROWS)
        if n + ahead < len(units):
            later, k = units[n + ahead]
            later(k).start()
    kept_blocks(low, kept)
    lane = lax.broadcasted_iota(jnp.int32, (8, LANES), 1)
    diagonal = (lane & 7) == lax.broadcasted_iota(jnp.int32, (8, LANES), 0)

    @pl.loop(0, out.shape[0], unroll=4)
    def _(i):
        gathered = jnp.zeros((8, LANES), jnp.float32)
        for g in range(LANES // 8):
            part = sums[pl.ds(pl.multiple_of(i * LANES + 8 * g, 8), 8), :]
            gathered = jnp.where((lane >> 3) == g, jnp.sum(part, axis=1, keepdims=True), gathered)
        out[pl.ds(i, 1), :] = -relax_factor * jnp.sum(
            jnp.where(diagonal, gathered, 0.0), axis=0, keepdims=True
        )

    @pl.when(w // ways == p)
    def _():
        own = pl.ds(lax.rem(w, ways) * height, height)
        out[...] += flat[own, :] + relax_factor * side[own, :]


def panel_kernel(wake_count, panel_count, *refs):
    blocks = refs[:panel_count]
    panels, plane, pairs = refs[panel_count : panel_count + 3]
    own_out = refs[panel_count + 3]
    outs = refs[panel_count + 4 : panel_count + 4 + wake_count]
    strengths, results, sources, spots, sides = refs[panel_count + 4 + wake_count :]
    w = lax.axis_index("wake")
    p = lax.axis_index("panel")
    value = blocks[0][...]
    for block in blocks[1:]:
        value = value + block[...]
    strengths[...] = value
    own = own_out.shape[0]
    own_out[...] = strengths[pl.ds(pl.multiple_of(p * own, own), own), :]
    tiles = strengths.shape[0]
    targets = plane.shape[1]
    for tile in range(tiles):
        at = slice(tile * LANES, (tile + 1) * LANES)
        for k in range(3):
            sources[k, tile] = jnp.broadcast_to(panels[k : k + 1, at], (8, LANES))
        area = panels[3:4, at]
        sources[3, tile] = jnp.broadcast_to(4.0 * area, (8, LANES))
        sources[4, tile] = jnp.broadcast_to(area * value[tile : tile + 1, :], (8, LANES))
    for tile in range(targets // LANES):
        at = slice(tile * LANES, (tile + 1) * LANES)
        turned = plane[:, at].T
        for k in range(3):
            spots[k, at, :] = jnp.broadcast_to(turned[:, k : k + 1], (LANES, LANES))
    lane = lax.broadcasted_iota(jnp.int32, (8, LANES), 1)
    zero = jnp.zeros((8, LANES), jnp.float32)
    deep = 4

    @pl.loop(0, targets // (8 * deep))
    def _(turn):
        rows = [pl.ds(pl.multiple_of((turn * deep + g) * 8, 8), 8) for g in range(deep)]
        spot = [[spots[k, at, :] for k in range(3)] for at in rows]

        def visit(tile, sums):
            sums = list(sums)
            cx, cy, cz, size, weight = (sources[k, tile] for k in range(5))
            for g in range(deep):
                dx = spot[g][0] - cx
                dy = spot[g][1] - cy
                dz = spot[g][2] - cz
                inverse = lax.rsqrt(dx * dx + dy * dy + (dz * dz + size))
                weighted = weight * inverse * (inverse * inverse)
                sums[3 * g] += weighted * dx
                sums[3 * g + 1] += weighted * dy
                sums[3 * g + 2] += weighted * dz
            return tuple(sums)

        sums = lax.fori_loop(0, tiles, visit, (zero,) * (3 * deep), unroll=math.gcd(tiles, 16))
        for g in range(deep):
            x, y, z = (jnp.sum(sums[3 * g + k], axis=1, keepdims=True) for k in range(3))
            sides[rows[g], :] = jnp.where(lane == 0, x, jnp.where(lane == 1, y, z))

    for tile in range(targets // LANES):
        at = slice(tile * LANES, (tile + 1) * LANES)
        turned = sides[at, :].T
        results[0:3, at] = inv_four_pi * (turned[0:3, :] - pairs[0:3, at])
    results[3:6, :] = -inv_four_pi * pairs[3:6, :]
    results[6:8, :] = jnp.zeros_like(pairs[6:8, :])
    nl = outs[0].shape[1]
    for j in range(wake_count):
        at = lax.rem(w + j, wake_count)
        outs[j][...] = results[:, pl.ds(pl.multiple_of(at * nl, LANES), nl)]


def final_kernel(count, *refs):
    parts, (velocity, stretching) = refs[:count], refs[count:]
    total = parts[0][...]
    for part in parts[1:]:
        total = total + part[...]
    for axis in range(3):
        velocity[axis : axis + 1, :] = total[axis : axis + 1, :] + freestream[axis]
    stretching[...] = total[3:6, :]


def block_device(
    positions,
    strengths,
    cores,
    panel_centers,
    panel_normals,
    panel_areas,
    influence,
    blade_ids,
    blade_velocity,
):
    wake_count = lax.axis_size("wake")
    panel_count = lax.axis_size("panel")
    ways = wake_count // panel_count
    nl = positions.shape[1]
    m = panel_centers.shape[1]
    rows, columns = influence.shape
    tiles = rows // LANES
    row_bytes = 4 * columns
    most = min(rows, KEEP_BYTES // row_bytes // LANES * LANES)
    counts = [most * share * MIB // KEEP_BYTES // RING_ROWS * RING_ROWS for share in SHARES]
    counts.append(most - sum(counts))
    parts = [(sum(counts[:i]), count) for i, count in enumerate(counts)]
    streamed = (most, rows - most)
    hold = pltpu.VMEM((most, columns), jnp.float32)
    route = functools.partial(send, wake_count=wake_count, panel_count=panel_count)

    particle, mixed = pl.pallas_call(
        pack_kernel,
        out_shape=(f32(8, nl), f32(8, m + nl)),
        in_specs=[hbm] * 8,
        out_specs=(vmem, vmem),
        scratch_shapes=[
            pltpu.VMEM((3, nl), jnp.float32),
            pltpu.VMEM((3, nl), jnp.float32),
            pltpu.VMEM((1, nl), jnp.float32),
            pltpu.VMEM((3, m), jnp.float32),
            pltpu.VMEM((3, m), jnp.float32),
            pltpu.VMEM((1, m), jnp.float32),
            pltpu.VMEM((1, m), jnp.int32),
            pltpu.SMEM(blade_velocity.shape, jnp.float32),
            pltpu.SemaphoreType.DMA((8,)),
        ],
        compiler_params=params(2),
    )(
        *(
            pltpu.with_memory_space_constraint(value, pltpu.HBM)
            for value in (
                positions,
                strengths,
                cores,
                panel_centers,
                panel_normals,
                panel_areas,
                blade_ids[None, :],
                blade_velocity,
            )
        )
    )
    lines = [mixed] + [
        route(mixed, route=lambda w, p, j=j: (w, partner(p, panel_count - j if panel_count & (panel_count - 1) else j, panel_count)))
        for j in range(1, panel_count)
    ]
    planes = [particle] + [
        route(particle, route=lambda w, p, j=j: ((w + j) % wake_count, p))
        for j in range(1, wake_count)
    ]
    keep = pl.pallas_call(
        functools.partial(load_kernel, *parts[0]),
        out_shape=hold,
        in_specs=[anywhere, hbm],
        out_specs=vmem,
        scratch_shapes=[pltpu.SemaphoreType.DMA],
        compiler_params=params(SCOPED),
    )(particle, influence)
    deep = math.gcd(wake_count * nl, 512)
    wide = 2 * LANES if rows % (2 * LANES) == 0 else LANES
    panels, plane, line, partial, keep = pl.pallas_call(
        functools.partial(wake_kernel, wake_count, panel_count, *parts[1]),
        out_shape=(
            f32(8, rows),
            f32(8, wake_count * nl),
            f32(8, panel_count * nl),
            f32(tiles, LANES),
            hold,
        ),
        in_specs=[anywhere] * (panel_count + wake_count) + [hbm, vmem],
        input_output_aliases={panel_count + wake_count + 1: 4},
        out_specs=(anywhere,) * 3 + (vmem,) * 2,
        scratch_shapes=[
            pltpu.VMEM((8, rows), jnp.float32),
            pltpu.VMEM((8, wake_count * nl), jnp.float32),
            pltpu.VMEM((8, panel_count * nl), jnp.float32),
            pltpu.VMEM((wake_count * nl, 48), jnp.bfloat16),
            pltpu.VMEM((48, rows), jnp.bfloat16),
            pltpu.VMEM((2, deep, wide), jnp.float32),
            pltpu.VMEM((4, wake_count * nl, LANES), jnp.float32),
            pltpu.VMEM((tiles, 8, LANES), jnp.float32),
            pltpu.SemaphoreType.DMA,
            pltpu.SemaphoreType.DMA((wake_count + 2 * panel_count + 3,)),
        ],
        compiler_params=params(max(SCOPED, 4 + wake_count * nl // 512)),
    )(*lines, *planes, influence, *stay(keep))

    def exchange(value):
        return [
            route(
                value,
                route=lambda w, p, j=j: (
                    (w % ways * panel_count + p + j) % wake_count,
                    w // ways,
                ),
            )
            for j in range(wake_count)
        ]

    def multiply(blocks, keep, side=None):
        opening = side is None
        outs = [near(tiles, LANES)]
        if opening:
            outs += [near(columns // LANES, LANES), hold]
        return pl.pallas_call(
            functools.partial(
                product_kernel, opening, wake_count, panel_count, parts[3], streamed
            ),
            out_shape=outs,
            in_specs=[vmem] * (wake_count + 1) + [hbm] + [vmem] * (not opening),
            out_specs=[vmem] * len(outs),
            input_output_aliases={wake_count: 2} if opening else {},
            scratch_shapes=[
                pltpu.VMEM((columns // LANES, 8, LANES), jnp.float32),
                pltpu.VMEM((columns // LANES, LANES), jnp.float32),
                pltpu.VMEM((rows, LANES), jnp.float32),
                pltpu.VMEM((RING, RING_ROWS, columns), jnp.float32),
                pltpu.SemaphoreType.DMA((RING + parts[3][1] // RING_ROWS,)),
            ],
            compiler_params=params(SCOPED),
        )(*stay(*blocks, keep), influence, *(() if opening else stay(side)))

    blocks = exchange(partial)
    pairs, keep = pl.pallas_call(
        functools.partial(pair_kernel, *parts[2]),
        out_shape=(f32(8, wake_count * nl), hold),
        in_specs=[anywhere, anywhere, hbm, vmem],
        out_specs=(vmem, vmem),
        input_output_aliases={3: 1},
        scratch_shapes=[
            pltpu.VMEM((8, wake_count * nl), jnp.float32),
            pltpu.VMEM((8, panel_count * nl), jnp.float32),
            pltpu.VMEM((panel_count * nl, 8), jnp.float32),
            pltpu.SemaphoreType.DMA,
            pltpu.SemaphoreType.DMA((2,)),
        ],
        compiler_params=params(SCOPED),
    )(plane, line, influence, *stay(keep))
    partial, right_side, keep = multiply(blocks, keep)
    for turn in range(ITERS - 2):
        (partial,) = multiply(exchange(partial), keep, right_side)
    ends = [partial] + [
        route(partial, route=lambda w, p, j=j: (w, partner(p, panel_count - j if panel_count & (panel_count - 1) else j, panel_count)))
        for j in range(1, panel_count)
    ]
    own, *sums = pl.pallas_call(
        functools.partial(panel_kernel, wake_count, panel_count),
        out_shape=(f32(m // LANES, LANES),) + (near(8, nl),) * wake_count,
        in_specs=[vmem] * (panel_count + 3),
        out_specs=(vmem,) * (1 + wake_count),
        scratch_shapes=[
            pltpu.VMEM((tiles, LANES), jnp.float32),
            pltpu.VMEM((8, wake_count * nl), jnp.float32),
            pltpu.VMEM((5, tiles, 8, LANES), jnp.float32),
            pltpu.VMEM((3, wake_count * nl, LANES), jnp.float32),
            pltpu.VMEM((wake_count * nl, LANES), jnp.float32),
        ],
        compiler_params=params(4 + wake_count * nl // 512),
    )(*ends, panels, plane, pairs)
    received = [sums[0]] + [
        route(sums[j], route=lambda w, p, j=j: ((w + j) % wake_count, p))
        for j in range(1, wake_count)
    ]
    velocity, stretching = pl.pallas_call(
        functools.partial(final_kernel, wake_count),
        out_shape=(f32(3, nl), f32(3, nl)),
        in_specs=[vmem] * wake_count,
        out_specs=(vmem, vmem),
        compiler_params=params(1),
    )(*stay(*received))
    return (velocity, stretching, own.reshape(m))


def fits(positions, panel_centers, influence):
    wake_count = lax.axis_size("wake")
    panel_count = lax.axis_size("panel")
    return (
        wake_count % panel_count == 0
        and positions.shape[1] % LANES == 0
        and wake_count * positions.shape[1] % (2 * LANES) == 0
        and panel_centers.shape[1] % LANES == 0
        and influence.shape[1] % (2 * LANES) == 0
    )


def per_device(*arrays):
    if fits(arrays[0], arrays[3], arrays[6]):
        return block_device(*arrays)
    return plain_device(*arrays)


def solution(mesh):
    in_specs = (
        P(None, ("groups", "wake", "panel")),
        P(None, ("groups", "wake", "panel")),
        P(None, ("groups", "wake", "panel")),
        P(None, ("groups", "wake", "panel")),
        P(None, ("groups", "wake", "panel")),
        P(None, ("groups", "wake", "panel")),
        P(("groups", "wake"), "panel"),
        P(("groups", "wake", "panel")),
        P("groups", None),
    )
    out_specs = (
        P(None, ("groups", "wake", "panel")),
        P(None, ("groups", "wake", "panel")),
        P(("groups", "wake", "panel")),
    )
    return jax.shard_map(
        per_device, mesh=mesh, in_specs=in_specs, out_specs=out_specs, check_vma=False
    )
```

```python
import functools
import math

import jax
import jax.numpy as jnp
from jax import lax
from jax.experimental import pallas as pl
from jax.experimental.pallas import tpu as pltpu
from jax.sharding import PartitionSpec as P

BLADES = 4
ITERS = 4


inv_four_pi = 1.0 / (4.0 * math.pi)
relax_factor = 0.5
freestream = (0.0, 0.0, -1.0)
block_width = 2048


def spread(block, axis, source):
    block = jnp.where(lax.axis_index(axis) == source, block, jnp.zeros_like(block))
    return lax.psum(block, axis)


def vortex_terms(targets, sources):
    target_pos, target_str, target_core = targets
    source_pos, source_str, source_core = sources
    offset_x = target_pos[0][:, None] - source_pos[0][None, :]
    offset_y = target_pos[1][:, None] - source_pos[1][None, :]
    offset_z = target_pos[2][:, None] - source_pos[2][None, :]
    core_sq = 0.5 * (
        target_core[0][:, None] * target_core[0][:, None]
        + source_core[0][None, :] * source_core[0][None, :]
    )
    distance = offset_x * offset_x + offset_y * offset_y + offset_z * offset_z + core_sq
    inverse = lax.rsqrt(distance)
    falloff = inverse * inverse * inverse
    steeper = falloff * inverse * inverse
    source_x = source_str[0][None, :]
    source_y = source_str[1][None, :]
    source_z = source_str[2][None, :]
    target_x = target_str[0][:, None]
    target_y = target_str[1][:, None]
    target_z = target_str[2][:, None]
    cross_x = offset_y * source_z - offset_z * source_y
    cross_y = offset_z * source_x - offset_x * source_z
    cross_z = offset_x * source_y - offset_y * source_x
    twist_x = target_y * source_z - target_z * source_y
    twist_y = target_z * source_x - target_x * source_z
    twist_z = target_x * source_y - target_y * source_x
    along = 3.0 * steeper * (target_x * offset_x + target_y * offset_y + target_z * offset_z)
    return jnp.stack(
        [
            jnp.sum(falloff * cross_x, axis=1),
            jnp.sum(falloff * cross_y, axis=1),
            jnp.sum(falloff * cross_z, axis=1),
            jnp.sum(falloff * twist_x - along * cross_x, axis=1),
            jnp.sum(falloff * twist_y - along * cross_y, axis=1),
            jnp.sum(falloff * twist_z - along * cross_z, axis=1),
        ]
    )


def wake_terms(targets, sources):
    points = targets[0]
    source_pos, source_str, source_core = sources
    offset_x = points[0][:, None] - source_pos[0][None, :]
    offset_y = points[1][:, None] - source_pos[1][None, :]
    offset_z = points[2][:, None] - source_pos[2][None, :]
    distance = (
        offset_x * offset_x
        + offset_y * offset_y
        + offset_z * offset_z
        + source_core[0][None, :] * source_core[0][None, :]
    )
    inverse = lax.rsqrt(distance)
    falloff = inverse * inverse * inverse
    source_x = source_str[0][None, :]
    source_y = source_str[1][None, :]
    source_z = source_str[2][None, :]
    return jnp.stack(
        [
            jnp.sum(falloff * (offset_y * source_z - offset_z * source_y), axis=1),
            jnp.sum(falloff * (offset_z * source_x - offset_x * source_z), axis=1),
            jnp.sum(falloff * (offset_x * source_y - offset_y * source_x), axis=1),
        ]
    )


def panel_terms(targets, sources):
    points = targets[0]
    centers, weights, areas = sources
    offset_x = points[0][:, None] - centers[0][None, :]
    offset_y = points[1][:, None] - centers[1][None, :]
    offset_z = points[2][:, None] - centers[2][None, :]
    distance = (
        offset_x * offset_x + offset_y * offset_y + offset_z * offset_z + 4.0 * areas[0][None, :]
    )
    inverse = lax.rsqrt(distance)
    weighted = weights[0][None, :] * inverse * inverse * inverse
    return jnp.stack(
        [
            jnp.sum(weighted * offset_x, axis=1),
            jnp.sum(weighted * offset_y, axis=1),
            jnp.sum(weighted * offset_z, axis=1),
        ]
    )


def over_sources(kernel, targets, sources, width, out_rows):
    length = sources[0].shape[-1]
    stride = math.gcd(length, width)
    if stride == length:
        return kernel(targets, sources)
    pieces = tuple(
        (
            jnp.moveaxis(source.reshape(source.shape[0], length // stride, stride), 1, 0)
            for source in sources
        )
    )

    def visit(running, entry):
        return (running + kernel(targets, entry), None)

    initial = jnp.zeros((out_rows, targets[0].shape[-1]), jnp.float32)
    running, unused = lax.scan(visit, initial, pieces)
    return running


def column_of(row_block):
    wake_count = lax.axis_size("wake")
    panel_count = lax.axis_size("panel")
    panel_at = lax.axis_index("panel")
    first_root = panel_at * wake_count // panel_count
    donors = max(1, wake_count // panel_count)
    pieces = []
    for offset_rank in range(donors):
        pieces.append(spread(row_block, "wake", first_root + offset_rank))
    joined = pieces[0] if donors == 1 else jnp.concatenate(pieces, axis=0)
    return joined


def relax(right_side, influence):
    row_side = lax.all_gather(right_side, "panel", axis=0, tiled=True)
    current = relax_factor * row_side
    for turn in range(ITERS - 1):
        column = column_of(current)
        partial_value = jnp.dot(influence, column, precision=lax.Precision.HIGHEST)
        image = lax.psum(partial_value, "panel")
        current = current + relax_factor * (row_side - image)
    own_start = lax.axis_index("panel") * right_side.shape[0]
    return lax.dynamic_slice_in_dim(current, own_start, right_side.shape[0], 0)


def plain_device(
    positions,
    strengths,
    cores,
    panel_centers,
    panel_normals,
    panel_areas,
    influence,
    blade_ids,
    blade_velocity,
):
    onset_dir = jnp.asarray(freestream, jnp.float32)[:, None]
    onehot = (blade_ids[None, :] == jnp.arange(BLADES, dtype=jnp.int32)[:, None]).astype(
        jnp.float32
    )
    kinematic = jnp.dot(blade_velocity.T, onehot, precision=lax.Precision.HIGHEST) + onset_dir
    moving = -jnp.sum(panel_normals * kinematic, axis=0)
    particles = (positions, strengths, cores)
    piece = (
        lax.all_gather(positions, ("wake", "panel"), axis=1, tiled=True),
        lax.all_gather(strengths, ("wake", "panel"), axis=1, tiled=True),
        lax.all_gather(cores, ("wake", "panel"), axis=1, tiled=True),
    )
    pair_sums = over_sources(vortex_terms, particles, piece, block_width, 6)
    wake_sums = over_sources(wake_terms, (panel_centers,), piece, block_width, 3)
    right_side = moving + inv_four_pi * jnp.sum(panel_normals * wake_sums, axis=0)
    centers, areas = (
        lax.all_gather(panel_centers, ("wake", "panel"), axis=1, tiled=True),
        lax.all_gather(panel_areas, ("wake", "panel"), axis=1, tiled=True),
    )
    panel_strengths = relax(right_side, influence)
    all_strengths = lax.all_gather(panel_strengths, ("wake", "panel"), axis=0, tiled=True)
    weights = (all_strengths * areas[0])[None, :]
    panel_sums = over_sources(panel_terms, (positions,), (centers, weights, areas), block_width, 3)
    velocity = onset_dir - inv_four_pi * pair_sums[:3] + inv_four_pi * panel_sums
    stretching = -inv_four_pi * pair_sums[3:]
    return (velocity, stretching, panel_strengths)


LANES = 128
MIB = 1 << 20
KEEP_BYTES = 50 * MIB
SHARES = (7, 23, 13)
SCOPED = 7
RING_ROWS = 64
RING = 4
AXES = ("wake", "panel")

vmem = pl.BlockSpec(memory_space=pltpu.VMEM)
hbm = pl.BlockSpec(memory_space=pltpu.HBM)
anywhere = pl.BlockSpec(memory_space=pl.ANY)


def f32(*shape):
    return jax.ShapeDtypeStruct(shape, jnp.float32)


def near(*shape):
    return pltpu.VMEM(shape, jnp.float32)


def stay(*values):
    return tuple(pltpu.with_memory_space_constraint(value, pltpu.VMEM) for value in values)


def params(mib):
    return pltpu.CompilerParams(vmem_limit_bytes=mib * MIB)


def send(value, wake_count, panel_count, route):
    pairs = []
    for w in range(wake_count):
        for p in range(panel_count):
            target = route(w, p)
            if target is not None:
                pairs.append((w * panel_count + p, target[0] * panel_count + target[1]))
    return lax.ppermute(value, AXES, pairs)


def partner(index, step, count):
    if count & (count - 1) == 0:
        return index ^ step
    return (index + count - step) % count


def pack_kernel(*refs):
    sources, (particle_out, mixed_out), held, sems = refs[:8], refs[8:10], refs[10:18], refs[18]
    copies = [
        pltpu.make_async_copy(source, target, sems.at[i])
        for i, (source, target) in enumerate(zip(sources, held))
    ]
    for copy in copies:
        copy.start()
    for copy in copies:
        copy.wait()
    positions, strengths, cores, centers, normals, areas, ids, blades = held
    particle_out[0:3, :] = positions[...]
    particle_out[3:6, :] = strengths[...]
    particle_out[6:7, :] = cores[...]
    particle_out[7:8, :] = jnp.zeros_like(cores[...])
    width = centers.shape[1]
    mixed_out[0:3, 0:width] = centers[...]
    mixed_out[3:4, 0:width] = areas[...]
    mixed_out[4:7, 0:width] = normals[...]
    owner = ids[...]
    total = None
    for axis in range(3):
        speed = jnp.zeros(owner.shape, jnp.float32)
        for blade in range(BLADES):
            speed = jnp.where(owner == blade, blades[blade, axis], speed)
        term = normals[axis : axis + 1, :] * (speed + freestream[axis])
        total = term if total is None else total + term
    mixed_out[7:8, 0:width] = -total
    mixed_out[:, width:] = particle_out[...]


def load_kernel(row, rows, after, influence, keep, sem):
    del after
    copy = pltpu.make_async_copy(
        influence.at[pl.ds(row, rows)], keep.at[pl.ds(row, rows)], sem
    )
    copy.start()
    copy.wait()


def thirds(value):
    high = value.astype(jnp.bfloat16).astype(jnp.float32)
    rest = value - high
    middle = rest.astype(jnp.bfloat16).astype(jnp.float32)
    return high, middle, rest - middle


def wake_kernel(wake_count, panel_count, row, rows, *refs):
    mixed = refs[:panel_count]
    planes = refs[panel_count : panel_count + wake_count]
    influence, _, panels_out, plane_out, line_out, partial_out, keep = refs[
        panel_count + wake_count :
    ][:7]
    panels, plane, line, left, right, product, spots, running, sem, sems = refs[
        panel_count + wake_count + 7 :
    ]
    w = lax.axis_index("wake")
    p = lax.axis_index("panel")
    nl = planes[0].shape[1]
    m = mixed[0].shape[1] - nl
    moves = []
    for j in range(wake_count):
        at = lax.rem(w + wake_count - j, wake_count)
        moves.append((planes[j], plane.at[:, pl.ds(pl.multiple_of(at * nl, LANES), nl)]))
    for j in range(panel_count):
        at = partner(p, j, panel_count)
        moves.append(
            (mixed[j].at[:, 0:m], panels.at[:, pl.ds(pl.multiple_of(at * m, LANES), m)])
        )
        moves.append(
            (mixed[j].at[:, m : m + nl], line.at[:, pl.ds(pl.multiple_of(at * nl, LANES), nl)])
        )
    moves = [
        pltpu.make_async_copy(source, target, sems.at[i])
        for i, (source, target) in enumerate(moves)
    ]
    for move in moves:
        move.start()
    for move in moves:
        move.wait()
    copy = pltpu.make_async_copy(
        influence.at[pl.ds(row, rows)], keep.at[pl.ds(row, rows)], sem
    )
    results = [
        pltpu.make_async_copy(source, target, sems.at[len(moves) + i])
        for i, (source, target) in enumerate(
            ((panels, panels_out), (plane, plane_out), (line, line_out))
        )
    ]
    for result in results:
        result.start()
    copy.start()
    count = plane.shape[1]
    targets = panels.shape[1]
    px, py, pz = (plane[k : k + 1, :] for k in range(3))
    sx, sy, sz = (plane[k : k + 1, :] for k in range(3, 6))
    blank = jnp.zeros((2, count), jnp.float32)
    source = jnp.concatenate(
        [sx, sy, sz, py * sz - pz * sy, pz * sx - px * sz, px * sy - py * sx, blank], axis=0
    )
    high, middle, low = thirds(source)
    left[...] = jnp.concatenate([high, high, middle, high, low, middle], axis=0).T.astype(
        jnp.bfloat16
    )
    cx, cy, cz = (panels[k : k + 1, :] for k in range(3))
    nx, ny, nz = (panels[k : k + 1, :] for k in range(4, 7))
    blank = jnp.zeros((2, targets), jnp.float32)
    target = jnp.concatenate(
        [ny * cz - nz * cy, nz * cx - nx * cz, nx * cy - ny * cx, -nx, -ny, -nz, blank], axis=0
    )
    high, middle, low = thirds(target)
    right[...] = jnp.concatenate([high, middle, high, low, high, middle], axis=0).astype(
        jnp.bfloat16
    )
    for tile in range(count // LANES):
        turned = plane[:, tile * LANES : (tile + 1) * LANES].T
        for k in range(3):
            spots[k, tile * LANES : (tile + 1) * LANES, :] = jnp.broadcast_to(
                turned[:, k : k + 1], (LANES, LANES)
            )
        spots[3, tile * LANES : (tile + 1) * LANES, :] = jnp.broadcast_to(
            turned[:, 6:7] * turned[:, 6:7], (LANES, LANES)
        )
    wide = product.shape[2]
    deep = product.shape[1]
    steps = count // deep
    total = targets // wide * steps

    def multiply(step, slot):
        column = lax.div(step, steps)
        block = lax.rem(step, steps)
        product[slot] = jnp.dot(
            left[pl.ds(pl.multiple_of(block * deep, deep), deep), :],
            right[:, pl.ds(pl.multiple_of(column * wide, wide), wide)],
            preferred_element_type=jnp.float32,
        )

    running[...] = jnp.zeros_like(running)
    multiply(0, 0)

    @pl.loop(0, total)
    def _(step):
        slot = lax.rem(step, 2)
        column = lax.div(step, steps)
        block = lax.rem(step, steps)
        multiply(jnp.minimum(step + 1, total - 1), 1 - slot)
        tiles = wide // LANES
        spot = []
        for t in range(tiles):
            lanes = pl.ds(pl.multiple_of(column * wide + t * LANES, LANES), LANES)
            spot.append(
                tuple(jnp.broadcast_to(panels[k : k + 1, lanes], (8, LANES)) for k in range(3))
            )
        sums = [jnp.zeros((8, LANES), jnp.float32)] * tiles
        for g in range(deep // 8):
            at = pl.ds(pl.multiple_of(block * deep + g * 8, 8), 8)
            qx, qy, qz, core = (spots[k, at, :] for k in range(4))
            for t in range(tiles):
                dx = spot[t][0] - qx
                dy = spot[t][1] - qy
                dz = spot[t][2] - qz
                inverse = lax.rsqrt(dx * dx + dy * dy + (dz * dz + core))
                falloff = inverse * inverse * inverse
                sums[t] = sums[t] + falloff * product[
                    slot, g * 8 : g * 8 + 8, t * LANES : (t + 1) * LANES
                ]
        for t in range(tiles):
            running[column * tiles + t] += sums[t]

    @pl.loop(0, targets // LANES)
    def _(tile):
        partial_out[pl.ds(tile, 1), :] = inv_four_pi * jnp.sum(running[tile], axis=0, keepdims=True)

    for tile in range(m // LANES):
        partial_out[pl.ds(p * (m // LANES) + tile, 1), :] += panels[
            7:8, pl.ds(pl.multiple_of(p * m + tile * LANES, LANES), LANES)
        ]
    for result in results:
        result.wait()
    copy.wait()


def pair_kernel(
    row, rows, plane_in, line_in, influence, held, out, keep, plane, line, turned, sem, sems
):
    del held
    moves = (
        pltpu.make_async_copy(plane_in, plane, sems.at[0]),
        pltpu.make_async_copy(line_in, line, sems.at[1]),
    )
    for move in moves:
        move.start()
    copy = pltpu.make_async_copy(
        influence.at[pl.ds(row, rows)], keep.at[pl.ds(row, rows)], sem
    )
    copy.start()
    for move in moves:
        move.wait()
    targets = plane.shape[1]
    sources = line.shape[1]
    for tile in range(sources // LANES):
        turned[tile * LANES : (tile + 1) * LANES, :] = line[
            :, tile * LANES : (tile + 1) * LANES
        ].T
    wide = 4 if targets % (4 * LANES) == 0 else 2

    @pl.loop(0, targets // (wide * LANES))
    def _(column):
        mine = []
        for t in range(wide):
            lanes = pl.ds(pl.multiple_of((column * wide + t) * LANES, LANES), LANES)
            mine.append([jnp.broadcast_to(plane[k : k + 1, lanes], (8, LANES)) for k in range(7)])
            mine[t][6] = 0.5 * (mine[t][6] * mine[t][6])

        def group(g, sums):
            rows = turned[pl.ds(pl.multiple_of(g * 8, 8), 8), :]
            sums = list(sums)
            other = [jnp.broadcast_to(rows[:, k : k + 1], (8, LANES)) for k in range(7)]
            half = 0.5 * (other[6] * other[6])
            for t in range(wide):
                tx, ty, tz, ux, uy, uz, core = mine[t]
                ox, oy, oz, sx, sy, sz, _ = other
                dx, dy, dz = tx - ox, ty - oy, tz - oz
                inverse = lax.rsqrt(dx * dx + dy * dy + dz * dz + (core + half))
                square = inverse * inverse
                falloff = square * inverse
                crosses = (dy * sz - dz * sy, dz * sx - dx * sz, dx * sy - dy * sx)
                twists = (uy * sz - uz * sy, uz * sx - ux * sz, ux * sy - uy * sx)
                along = 3.0 * square * (ux * dx + uy * dy + uz * dz)
                for k in range(3):
                    sums[6 * t + k] += falloff * crosses[k]
                    sums[6 * t + 3 + k] += falloff * (twists[k] - along * crosses[k])
            return tuple(sums)

        zero = jnp.zeros((8, LANES), jnp.float32)
        sums = lax.fori_loop(0, sources // 8, group, (zero,) * (6 * wide), unroll=4)
        for t in range(wide):
            lanes = pl.ds(pl.multiple_of((column * wide + t) * LANES, LANES), LANES)
            for k in range(6):
                out[k : k + 1, lanes] = jnp.sum(sums[6 * t + k], axis=0, keepdims=True)
            out[6:8, lanes] = jnp.zeros((2, LANES), jnp.float32)

    copy.wait()


def product_kernel(opening, wake_count, panel_count, fresh, streamed, *refs):
    refs = list(refs)
    take = lambda count: [refs.pop(0) for _ in range(count)]
    blocks = take(wake_count)
    keep, influence = take(2)
    if opening:
        out, side, keep = take(3)
    else:
        side, out = take(2)
    column, flat, sums, ring, sem = take(5)
    first, rows = streamed
    chunks = rows // RING_ROWS
    extra = fresh[1] // RING_ROWS if opening else 0
    kept = (fresh[0] if opening else first) // RING_ROWS

    def fetch(i):
        return pltpu.make_async_copy(
            influence.at[pl.ds(first + i * RING_ROWS, RING_ROWS)],
            ring.at[i % RING],
            sem.at[i % RING],
        )

    def settle(i):
        return pltpu.make_async_copy(
            influence.at[pl.ds(fresh[0] + i * RING_ROWS, RING_ROWS)],
            keep.at[pl.ds(fresh[0] + i * RING_ROWS, RING_ROWS)],
            sem.at[RING + i],
        )

    units = [((i + 0.5) / chunks, fetch, i) for i in range(chunks)]
    units += [((i + 0.5) / extra, settle, i) for i in range(extra)]
    units = [unit[1:] for unit in sorted(units, key=lambda unit: unit[0])]
    ahead = RING + 2 if extra else RING
    if any(
        sum(unit[0] is fetch for unit in units[i : i + ahead]) > RING for i in range(len(units))
    ):
        ahead = RING
    for copy, i in units[:ahead]:
        copy(i).start()
    w = lax.axis_index("wake")
    p = lax.axis_index("panel")
    ways = wake_count // panel_count
    height = blocks[0].shape[0]
    for e in range(ways):
        value = None
        for j in range(wake_count):
            term = blocks[j][...]
            if ways > 1:
                sender = lax.rem(w + wake_count - j, wake_count)
                term = jnp.where(sender // panel_count == e, term, 0.0)
            value = term if value is None else value + term
        if opening:
            side[e * height : (e + 1) * height, :] = value
            value = relax_factor * value
        flat[e * height : (e + 1) * height, :] = value
        for k in range(height):
            column[e * height + k] = jnp.broadcast_to(value[k : k + 1, :], (8, LANES))
    tiles = column.shape[0]
    vectors = [column[k] for k in range(tiles)]

    def block(ref, start, at, height):
        for g in range(height // 8):
            even = odd = None
            for k in range(0, tiles, 2):
                a = ref[pl.ds(start + 8 * g, 8), k * LANES : (k + 1) * LANES] * vectors[k]
                b = ref[pl.ds(start + 8 * g, 8), (k + 1) * LANES : (k + 2) * LANES] * vectors[k + 1]
                even = a if even is None else even + a
                odd = b if odd is None else odd + b
            sums[pl.ds(at + 8 * g, 8), :] = even + odd

    def kept_blocks(low, high):
        if high > low:

            @pl.loop(low, high)
            def _(i):
                at = pl.multiple_of(i * RING_ROWS, RING_ROWS)
                block(keep, at, at, RING_ROWS)

    low = 0
    for n, (copy, i) in enumerate(units):
        high = kept * (n + 1) // (len(units) + 1)
        kept_blocks(low, high)
        low = high
        copy(i).wait()
        if copy is fetch:
            block(ring.at[i % RING], 0, first + i * RING_ROWS, RING_ROWS)
        else:
            at = fresh[0] + i * RING_ROWS
            block(keep, at, at, RING_ROWS)
        if n + ahead < len(units):
            later, k = units[n + ahead]
            later(k).start()
    kept_blocks(low, kept)
    lane = lax.broadcasted_iota(jnp.int32, (8, LANES), 1)
    diagonal = (lane & 7) == lax.broadcasted_iota(jnp.int32, (8, LANES), 0)

    @pl.loop(0, out.shape[0], unroll=4)
    def _(i):
        gathered = jnp.zeros((8, LANES), jnp.float32)
        for g in range(LANES // 8):
            part = sums[pl.ds(pl.multiple_of(i * LANES + 8 * g, 8), 8), :]
            gathered = jnp.where((lane >> 3) == g, jnp.sum(part, axis=1, keepdims=True), gathered)
        out[pl.ds(i, 1), :] = -relax_factor * jnp.sum(
            jnp.where(diagonal, gathered, 0.0), axis=0, keepdims=True
        )

    @pl.when(w // ways == p)
    def _():
        own = pl.ds(lax.rem(w, ways) * height, height)
        out[...] += flat[own, :] + relax_factor * side[own, :]


def panel_kernel(wake_count, panel_count, *refs):
    blocks = refs[:panel_count]
    panels, plane, pairs = refs[panel_count : panel_count + 3]
    own_out = refs[panel_count + 3]
    outs = refs[panel_count + 4 : panel_count + 4 + wake_count]
    strengths, results, sources, spots, sides = refs[panel_count + 4 + wake_count :]
    w = lax.axis_index("wake")
    p = lax.axis_index("panel")
    value = blocks[0][...]
    for block in blocks[1:]:
        value = value + block[...]
    strengths[...] = value
    own = own_out.shape[0]
    own_out[...] = strengths[pl.ds(pl.multiple_of(p * own, own), own), :]
    tiles = strengths.shape[0]
    targets = plane.shape[1]
    for tile in range(tiles):
        at = slice(tile * LANES, (tile + 1) * LANES)
        for k in range(3):
            sources[k, tile] = jnp.broadcast_to(panels[k : k + 1, at], (8, LANES))
        area = panels[3:4, at]
        sources[3, tile] = jnp.broadcast_to(4.0 * area, (8, LANES))
        sources[4, tile] = jnp.broadcast_to(area * value[tile : tile + 1, :], (8, LANES))
    for tile in range(targets // LANES):
        at = slice(tile * LANES, (tile + 1) * LANES)
        turned = plane[:, at].T
        for k in range(3):
            spots[k, at, :] = jnp.broadcast_to(turned[:, k : k + 1], (LANES, LANES))
    lane = lax.broadcasted_iota(jnp.int32, (8, LANES), 1)
    zero = jnp.zeros((8, LANES), jnp.float32)
    deep = 4

    @pl.loop(0, targets // (8 * deep))
    def _(turn):
        rows = [pl.ds(pl.multiple_of((turn * deep + g) * 8, 8), 8) for g in range(deep)]
        spot = [[spots[k, at, :] for k in range(3)] for at in rows]

        def visit(tile, sums):
            sums = list(sums)
            cx, cy, cz, size, weight = (sources[k, tile] for k in range(5))
            for g in range(deep):
                dx = spot[g][0] - cx
                dy = spot[g][1] - cy
                dz = spot[g][2] - cz
                inverse = lax.rsqrt(dx * dx + dy * dy + (dz * dz + size))
                weighted = weight * inverse * (inverse * inverse)
                sums[3 * g] += weighted * dx
                sums[3 * g + 1] += weighted * dy
                sums[3 * g + 2] += weighted * dz
            return tuple(sums)

        sums = lax.fori_loop(0, tiles, visit, (zero,) * (3 * deep), unroll=math.gcd(tiles, 16))
        for g in range(deep):
            x, y, z = (jnp.sum(sums[3 * g + k], axis=1, keepdims=True) for k in range(3))
            sides[rows[g], :] = jnp.where(lane == 0, x, jnp.where(lane == 1, y, z))

    for tile in range(targets // LANES):
        at = slice(tile * LANES, (tile + 1) * LANES)
        turned = sides[at, :].T
        results[0:3, at] = inv_four_pi * (turned[0:3, :] - pairs[0:3, at])
    results[3:6, :] = -inv_four_pi * pairs[3:6, :]
    results[6:8, :] = jnp.zeros_like(pairs[6:8, :])
    nl = outs[0].shape[1]
    for j in range(wake_count):
        at = lax.rem(w + j, wake_count)
        outs[j][...] = results[:, pl.ds(pl.multiple_of(at * nl, LANES), nl)]


def final_kernel(count, *refs):
    parts, (velocity, stretching) = refs[:count], refs[count:]
    total = parts[0][...]
    for part in parts[1:]:
        total = total + part[...]
    for axis in range(3):
        velocity[axis : axis + 1, :] = total[axis : axis + 1, :] + freestream[axis]
    stretching[...] = total[3:6, :]


def block_device(
    positions,
    strengths,
    cores,
    panel_centers,
    panel_normals,
    panel_areas,
    influence,
    blade_ids,
    blade_velocity,
):
    wake_count = lax.axis_size("wake")
    panel_count = lax.axis_size("panel")
    ways = wake_count // panel_count
    nl = positions.shape[1]
    m = panel_centers.shape[1]
    rows, columns = influence.shape
    tiles = rows // LANES
    row_bytes = 4 * columns
    most = min(rows, KEEP_BYTES // row_bytes // LANES * LANES)
    counts = [most * share * MIB // KEEP_BYTES // RING_ROWS * RING_ROWS for share in SHARES]
    counts.append(most - sum(counts))
    parts = [(sum(counts[:i]), count) for i, count in enumerate(counts)]
    streamed = (most, rows - most)
    hold = pltpu.VMEM((most, columns), jnp.float32)
    route = functools.partial(send, wake_count=wake_count, panel_count=panel_count)

    particle, mixed = pl.pallas_call(
        pack_kernel,
        out_shape=(f32(8, nl), f32(8, m + nl)),
        in_specs=[hbm] * 8,
        out_specs=(vmem, vmem),
        scratch_shapes=[
            pltpu.VMEM((3, nl), jnp.float32),
            pltpu.VMEM((3, nl), jnp.float32),
            pltpu.VMEM((1, nl), jnp.float32),
            pltpu.VMEM((3, m), jnp.float32),
            pltpu.VMEM((3, m), jnp.float32),
            pltpu.VMEM((1, m), jnp.float32),
            pltpu.VMEM((1, m), jnp.int32),
            pltpu.SMEM(blade_velocity.shape, jnp.float32),
            pltpu.SemaphoreType.DMA((8,)),
        ],
        compiler_params=params(2),
    )(
        *(
            pltpu.with_memory_space_constraint(value, pltpu.HBM)
            for value in (
                positions,
                strengths,
                cores,
                panel_centers,
                panel_normals,
                panel_areas,
                blade_ids[None, :],
                blade_velocity,
            )
        )
    )
    lines = [mixed] + [
        route(mixed, route=lambda w, p, j=j: (w, partner(p, panel_count - j if panel_count & (panel_count - 1) else j, panel_count)))
        for j in range(1, panel_count)
    ]
    planes = [particle] + [
        route(particle, route=lambda w, p, j=j: ((w + j) % wake_count, p))
        for j in range(1, wake_count)
    ]
    keep = pl.pallas_call(
        functools.partial(load_kernel, *parts[0]),
        out_shape=hold,
        in_specs=[anywhere, hbm],
        out_specs=vmem,
        scratch_shapes=[pltpu.SemaphoreType.DMA],
        compiler_params=params(SCOPED),
    )(particle, influence)
    deep = math.gcd(wake_count * nl, 512)
    wide = 2 * LANES if rows % (2 * LANES) == 0 else LANES
    panels, plane, line, partial, keep = pl.pallas_call(
        functools.partial(wake_kernel, wake_count, panel_count, *parts[1]),
        out_shape=(
            f32(8, rows),
            f32(8, wake_count * nl),
            f32(8, panel_count * nl),
            f32(tiles, LANES),
            hold,
        ),
        in_specs=[anywhere] * (panel_count + wake_count) + [hbm, vmem],
        input_output_aliases={panel_count + wake_count + 1: 4},
        out_specs=(anywhere,) * 3 + (vmem,) * 2,
        scratch_shapes=[
            pltpu.VMEM((8, rows), jnp.float32),
            pltpu.VMEM((8, wake_count * nl), jnp.float32),
            pltpu.VMEM((8, panel_count * nl), jnp.float32),
            pltpu.VMEM((wake_count * nl, 48), jnp.bfloat16),
            pltpu.VMEM((48, rows), jnp.bfloat16),
            pltpu.VMEM((2, deep, wide), jnp.float32),
            pltpu.VMEM((4, wake_count * nl, LANES), jnp.float32),
            pltpu.VMEM((tiles, 8, LANES), jnp.float32),
            pltpu.SemaphoreType.DMA,
            pltpu.SemaphoreType.DMA((wake_count + 2 * panel_count + 3,)),
        ],
        compiler_params=params(max(SCOPED, 4 + wake_count * nl // 512)),
    )(*lines, *planes, influence, *stay(keep))

    def exchange(value):
        sent = [
            route(
                value,
                route=lambda w, p, j=j: (
                    (w % ways * panel_count + p + j) % wake_count,
                    w // ways,
                ),
            )
            for j in reversed(range(wake_count))
        ]
        return sent[::-1]

    def multiply(blocks, keep, side=None):
        opening = side is None
        outs = [near(tiles, LANES)]
        if opening:
            outs += [near(columns // LANES, LANES), hold]
        return pl.pallas_call(
            functools.partial(
                product_kernel, opening, wake_count, panel_count, parts[3], streamed
            ),
            out_shape=outs,
            in_specs=[vmem] * (wake_count + 1) + [hbm] + [vmem] * (not opening),
            out_specs=[vmem] * len(outs),
            input_output_aliases={wake_count: 2} if opening else {},
            scratch_shapes=[
                pltpu.VMEM((columns // LANES, 8, LANES), jnp.float32),
                pltpu.VMEM((columns // LANES, LANES), jnp.float32),
                pltpu.VMEM((rows, LANES), jnp.float32),
                pltpu.VMEM((RING, RING_ROWS, columns), jnp.float32),
                pltpu.SemaphoreType.DMA((RING + parts[3][1] // RING_ROWS,)),
            ],
            compiler_params=params(SCOPED),
        )(*stay(*blocks, keep), influence, *(() if opening else stay(side)))

    blocks = exchange(partial)
    pairs, keep = pl.pallas_call(
        functools.partial(pair_kernel, *parts[2]),
        out_shape=(f32(8, wake_count * nl), hold),
        in_specs=[anywhere, anywhere, hbm, vmem],
        out_specs=(vmem, vmem),
        input_output_aliases={3: 1},
        scratch_shapes=[
            pltpu.VMEM((8, wake_count * nl), jnp.float32),
            pltpu.VMEM((8, panel_count * nl), jnp.float32),
            pltpu.VMEM((panel_count * nl, 8), jnp.float32),
            pltpu.SemaphoreType.DMA,
            pltpu.SemaphoreType.DMA((2,)),
        ],
        compiler_params=params(SCOPED),
    )(plane, line, influence, *stay(keep))
    partial, right_side, keep = multiply(blocks, keep)
    for turn in range(ITERS - 2):
        (partial,) = multiply(exchange(partial), keep, right_side)
    ends = [partial] + [
        route(partial, route=lambda w, p, j=j: (w, partner(p, panel_count - j if panel_count & (panel_count - 1) else j, panel_count)))
        for j in range(1, panel_count)
    ]
    own, *sums = pl.pallas_call(
        functools.partial(panel_kernel, wake_count, panel_count),
        out_shape=(f32(m // LANES, LANES),) + (near(8, nl),) * wake_count,
        in_specs=[vmem] * (panel_count + 3),
        out_specs=(vmem,) * (1 + wake_count),
        scratch_shapes=[
            pltpu.VMEM((tiles, LANES), jnp.float32),
            pltpu.VMEM((8, wake_count * nl), jnp.float32),
            pltpu.VMEM((5, tiles, 8, LANES), jnp.float32),
            pltpu.VMEM((3, wake_count * nl, LANES), jnp.float32),
            pltpu.VMEM((wake_count * nl, LANES), jnp.float32),
        ],
        compiler_params=params(4 + wake_count * nl // 512),
    )(*ends, panels, plane, pairs)
    received = [sums[0]] + [
        route(sums[j], route=lambda w, p, j=j: ((w + j) % wake_count, p))
        for j in range(1, wake_count)
    ]
    velocity, stretching = pl.pallas_call(
        functools.partial(final_kernel, wake_count),
        out_shape=(f32(3, nl), f32(3, nl)),
        in_specs=[vmem] * wake_count,
        out_specs=(vmem, vmem),
        compiler_params=params(1),
    )(*stay(*received))
    return (velocity, stretching, own.reshape(m))


def fits(positions, panel_centers, influence):
    wake_count = lax.axis_size("wake")
    panel_count = lax.axis_size("panel")
    return (
        wake_count % panel_count == 0
        and positions.shape[1] % LANES == 0
        and wake_count * positions.shape[1] % (2 * LANES) == 0
        and panel_centers.shape[1] % LANES == 0
        and influence.shape[1] % (2 * LANES) == 0
    )


def per_device(*arrays):
    if fits(arrays[0], arrays[3], arrays[6]):
        return block_device(*arrays)
    return plain_device(*arrays)


def solution(mesh):
    in_specs = (
        P(None, ("groups", "wake", "panel")),
        P(None, ("groups", "wake", "panel")),
        P(None, ("groups", "wake", "panel")),
        P(None, ("groups", "wake", "panel")),
        P(None, ("groups", "wake", "panel")),
        P(None, ("groups", "wake", "panel")),
        P(("groups", "wake"), "panel"),
        P(("groups", "wake", "panel")),
        P("groups", None),
    )
    out_specs = (
        P(None, ("groups", "wake", "panel")),
        P(None, ("groups", "wake", "panel")),
        P(("groups", "wake", "panel")),
    )
    return jax.shard_map(
        per_device, mesh=mesh, in_specs=in_specs, out_specs=out_specs, check_vma=False
    )
```
